32 devices in a mesh: row: 8 (over y, x, core), col: 4 (over z).
Axes of the slice: x: 2, y: 2, z: 4, core: 2. Of those that a mesh axis runs over, the one named last changes fastest.
Arguments:
- relu21_preact: bfloat16 [256, 256, 128], P('row', 'col'), may hold values from -6 to 6
- relu22_preact: bfloat16 [256, 256, 128], P('row', 'col'), may hold values from -600 to 600
- relu31_preact: bfloat16 [128, 128, 256], P('row', 'col'), may hold values from -6 to 6
- relu32_preact: bfloat16 [128, 128, 256], P('row', 'col'), may hold values from -6 to 6
- relu33_preact: bfloat16 [128, 128, 256], P('row', 'col'), may hold values from -600 to 600
- target22_preact: bfloat16 [256, 256, 128], P('row', 'col'), may hold values from -600 to 600
- target33_preact: bfloat16 [128, 128, 256], P('row', 'col'), may hold values from -600 to 600
- pool1_argmax: int32 [256, 16384], P('row', 'col'), may hold values from 0 to 3
- pool2_argmax: int32 [128, 16384], P('row', 'col'), may hold values from 0 to 3
- linear2_weight: float32 [128], replicated, may hold values from 0.2 to 2
- linear3_weight: float32 [256], replicated, may hold values from 0.2 to 2
- kernel21: bfloat16 [128, 576], replicated, may hold values from -0.25 to 0.25
- kernel22: bfloat16 [128, 1152], replicated, may hold values from -0.1875 to 0.1875
- kernel31: bfloat16 [256, 1152], replicated, may hold values from -0.1875 to 0.1875
- kernel32: bfloat16 [256, 2304], replicated, may hold values from -0.125 to 0.125
- kernel33: bfloat16 [256, 2304], replicated, may hold values from -0.125 to 0.125
Outputs:
- relu12_gradient: bfloat16 [512, 32768], P('row', 'col')
The draws below stay inside these ranges and needn't reach their ends.
Inputs may be any that keep to these rules, and one draw needn't show every extreme that they name: `pool1_argmax`: the position of the maximum in each 2x2 window, 0 top left, 1 top right, 2 bottom left, 3 bottom right; entry [r, c * 64 + ch] belongs to pooled cell (r, c) and channel ch. `pool2_argmax`: as for pool1_argmax, with 128 channels.
All inputs are finite; a program needn't handle non-finite values.
Results may differ from the reference program's by a relative error of at most 0.0059.
Values may be sent and summed in bfloat16 or wider, within the bound.
A program may use at most 64 MiB of HBM per device.

```python
import math
import jax
import jax.numpy as jnp
from jax import lax

CH1 = 64
CH2 = 128
CH3 = 256
HEIGHT = 128
WIDTH = 128


def tap_values(key, salt, height, breadth, channels):
    folded = jax.random.fold_in(key, salt)
    streams = jax.random.split(folded, 3)
    spread = math.log(10.0)
    values = jnp.clip(jax.random.normal(streams[2], (height, breadth, channels), jnp.float32), -4.0, 4.0)
    channel_scale = jnp.exp(jax.random.uniform(streams[0], (channels,), jnp.float32, 0.0, spread))
    pixel_scale = jnp.exp(jax.random.uniform(streams[1], (height, breadth, 1), jnp.float32, 0.0, spread))
    return (values * channel_scale * pixel_scale).astype(jnp.bfloat16)


def draw_relu22_preact(key, part):
    return tap_values(key, 11, 2 * HEIGHT, 2 * WIDTH, CH2)


def draw_relu33_preact(key, part):
    return tap_values(key, 12, HEIGHT, WIDTH, CH3)


def draw_target22_preact(key, part):
    return tap_values(key, 13, 2 * HEIGHT, 2 * WIDTH, CH2)


def draw_target33_preact(key, part):
    return tap_values(key, 14, HEIGHT, WIDTH, CH3)


def plant(drawn, own_key, least, top_value):
    index_at = [jax.random.randint(jax.random.fold_in(own_key, axis), (), 0, length) for axis, length in enumerate(drawn.shape)]
    longest = drawn.shape.index(max(drawn.shape))
    next_to = index_at[:longest] + [(index_at[longest] + 1) % drawn.shape[longest]] + index_at[longest + 1:]
    return drawn.at[tuple(index_at)].set(least).at[tuple(next_to)].set(top_value)


def levels(stream_key, dims, cuts, smallest, high):
    def one(dim, shards_of):
        draws = jax.random.uniform(jax.random.fold_in(jax.random.fold_in(stream_key, 6), dim), (shards_of,), jnp.float32, smallest / len(cuts), high / len(cuts))
        return jnp.repeat(jnp.exp(draws), dims[dim] // shards_of).reshape((-1,) + (1,) * (len(dims) - dim - 1))

    gain = one(*cuts[0])
    for cut in cuts[1:]:
        gain = gain * one(*cut)
    return gain


def centred(rng, shape, scale, limit, cuts=(), held_as=jnp.bfloat16):
    entries = scale * jax.random.normal(rng, shape, jnp.float32)
    if cuts:
        entries = entries * levels(rng, shape, cuts, -0.22, 0.18)
    return jnp.clip(entries, -limit, limit).astype(held_as)


def setup_inputs(seed: int = 0) -> dict:
    splits = jax.random.split(jax.random.key(seed), 17)
    return {
        "relu21_preact": centred(splits[0], (2 * HEIGHT, 2 * WIDTH, CH2), 1.0, 6.0, ((0, 8), (1, 4))),
        "relu22_preact": draw_relu22_preact(jax.random.fold_in(splits[16], 71), 0),
        "relu31_preact": centred(splits[2], (HEIGHT, WIDTH, CH3), 1.0, 6.0, ((0, 8), (1, 4))),
        "relu32_preact": centred(splits[3], (HEIGHT, WIDTH, CH3), 1.0, 6.0, ((0, 8), (1, 4))),
        "relu33_preact": draw_relu33_preact(jax.random.fold_in(splits[16], 71), 0),
        "target22_preact": draw_target22_preact(jax.random.fold_in(splits[16], 71), 0),
        "target33_preact": draw_target33_preact(jax.random.fold_in(splits[16], 71), 0),
        "pool1_argmax": plant(jax.random.randint(splits[7], (2 * HEIGHT, 2 * WIDTH * CH1), 0, 4), jax.random.fold_in(splits[7], 1), 0, 3).astype(jnp.int32),
        "pool2_argmax": plant(jax.random.randint(splits[8], (HEIGHT, WIDTH * CH2), 0, 4), jax.random.fold_in(splits[8], 1), 0, 3).astype(jnp.int32),
        "linear2_weight": jnp.clip(jnp.exp(jax.random.uniform(splits[9], (CH2,), jnp.float32, math.log(0.2), math.log(2.0))), 0.2, 2.0),
        "linear3_weight": jnp.clip(jnp.exp(jax.random.uniform(splits[10], (CH3,), jnp.float32, math.log(0.2), math.log(2.0))), 0.2, 2.0),
        "kernel21": centred(splits[11], (CH2, 9 * CH1), (9 * CH1) ** -0.5, 0.25),
        "kernel22": centred(splits[12], (CH2, 9 * CH2), (9 * CH2) ** -0.5, 0.1875),
        "kernel31": centred(splits[13], (CH3, 9 * CH2), (9 * CH2) ** -0.5, 0.1875),
        "kernel32": centred(splits[14], (CH3, 9 * CH3), (9 * CH3) ** -0.5, 0.125),
        "kernel33": centred(splits[15], (CH3, 9 * CH3), (9 * CH3) ** -0.5, 0.125),
    }


EPSILON = 1e-06

def inject(preact, target, weight):
    feature = jnp.maximum(preact.astype(jnp.float32), 0.0)
    wanted = jnp.maximum(target.astype(jnp.float32), 0.0)
    feature_norm = jnp.sqrt(lax.optimization_barrier(jnp.mean(feature * feature, axis=-1, keepdims=True)) + EPSILON)
    wanted_norm = jnp.sqrt(lax.optimization_barrier(jnp.mean(wanted * wanted, axis=-1, keepdims=True)) + EPSILON)
    scaled = feature / feature_norm
    excess = 2.0 * weight * (scaled - wanted / wanted_norm)
    return (excess - scaled * lax.optimization_barrier(jnp.mean(excess * scaled, axis=-1, keepdims=True))) / feature_norm

def masked(preact, values):
    return jnp.where(preact > 0, values, 0.0).astype(jnp.bfloat16)

def unpool(values, argmax_rows):
    height, breadth, channels = values.shape
    position = argmax_rows.reshape(height, breadth, channels)
    stripes = []
    for vertical in range(2):
        halves = [jnp.where(position == 2 * vertical + lateral, values, 0.0) for lateral in range(2)]
        stripes.append(jnp.stack(halves, axis=2))
    return jnp.stack(stripes, axis=1).reshape(2 * height, 2 * breadth, channels)

def back_conv(gradient, kernel):
    outputs = kernel.shape[0]
    channels_in = kernel.shape[1] // 9
    flipped = kernel.reshape(outputs, 3, 3, channels_in)[:, ::-1, ::-1, :]
    flipped = flipped.transpose(1, 2, 0, 3).astype(jnp.float32)
    result = lax.conv_general_dilated(gradient.astype(jnp.float32)[None], flipped, (1, 1), 'SAME', dimension_numbers=('NHWC', 'HWIO', 'NHWC'), precision=lax.Precision.HIGHEST)
    return result[0]

def reference(relu21_preact, relu22_preact, relu31_preact, relu32_preact, relu33_preact, target22_preact, target33_preact, pool1_argmax, pool2_argmax, linear2_weight, linear3_weight, kernel21, kernel22, kernel31, kernel32, kernel33):
    seeded = masked(relu33_preact, inject(relu33_preact, target33_preact, linear3_weight))
    gradient32 = masked(relu32_preact, back_conv(seeded, kernel33))
    gradient31 = masked(relu31_preact, back_conv(gradient32, kernel32))
    pooled2 = back_conv(gradient31, kernel31)
    arriving = unpool(pooled2, pool2_argmax) + inject(relu22_preact, target22_preact, linear2_weight)
    gradient22 = masked(relu22_preact, arriving)
    gradient21 = masked(relu21_preact, back_conv(gradient22, kernel22))
    pooled1 = back_conv(gradient21, kernel21)
    result = unpool(pooled1, pool1_argmax).astype(jnp.bfloat16)
    return result.reshape(result.shape[0], -1)
```

```python
import functools

import jax
import jax.numpy as jnp
from jax import lax
from jax.experimental import pallas as pl
from jax.experimental.pallas import tpu as pltpu
from jax.sharding import PartitionSpec as P

EPSILON = 1e-06
MESH = pl.DeviceIdType.MESH
F32 = jnp.float32
BF16 = jnp.bfloat16
SIDE = 8
OFF3 = 6
OFF2 = 4
OFFU = 2
PITCH = 17
DIRS = ((-1, 0), (1, 0), (0, -1), (0, 1), (-1, -1), (-1, 1), (1, -1), (1, 1))


WIDTHS = (4, 4, 2, 2, 2, 1)
ROWS = (4, 3, 2, 2, 2, 1)


def reachable(axes, counts, d, sign):
    checks = []
    for axis, count, step in zip(axes, counts, d):
        if step:
            target = lax.axis_index(axis) + sign * step
            checks.append(target >= 0 if sign * step < 0 else target < count)
    ok = checks[0]
    for c in checks[1:]:
        ok = jnp.logical_and(ok, c)
    return ok


def packed(tiles, width, side):
    k = SIDE // width
    rows, _, c = tiles.shape
    grouped = tiles.reshape(rows // k, k, SIDE, c)
    sub = lax.broadcasted_iota(jnp.int32, (rows // k, SIDE, c), 1)
    total = None
    for i in range(k):
        shift = (i * width - (0 if side == 0 else SIDE - width)) % SIDE
        piece = grouped[:, i]
        if shift:
            piece = pltpu.roll(piece, shift, 1)
        total = piece if total is None else jnp.where(sub >= i * width, piece, total)
    return total


def unpacked(tiles, width, side):
    k = SIDE // width
    count, _, c = tiles.shape
    pieces = []
    for i in range(k):
        shift = ((0 if side == 0 else SIDE - width) - i * width) % SIDE
        pieces.append(pltpu.roll(tiles, shift, 1) if shift else tiles)
    return jnp.stack(pieces, axis=1).reshape(count * k, SIDE, c)


def injected(p, t, weight):
    f = jnp.maximum(p, 0.0)
    g = jnp.maximum(t, 0.0)
    rinv = lax.rsqrt(jnp.mean(f * f, axis=-1, keepdims=True) + EPSILON)
    sinv = lax.rsqrt(jnp.mean(g * g, axis=-1, keepdims=True) + EPSILON)
    u = f * rinv
    e = weight * (u - g * sinv)
    return (e - u * jnp.mean(e * u, axis=-1, keepdims=True)) * rinv


def row_shifts(z, stride, n):
    z = z.reshape(-1, stride, 3 * n)
    return pltpu.roll(z[:, :, :n], stride - 1, 1) + z[:, :, n : 2 * n] + pltpu.roll(z[:, :, 2 * n :], 1, 1)


def conv_rows(x, w, first, rows, stride, n):
    parts = [x[(first + 1 - dy) * stride : (first + 1 - dy + rows) * stride, :] for dy in range(3)]
    z = jnp.dot(jnp.concatenate(parts, axis=1), w[...], preferred_element_type=F32)
    return row_shifts(z, stride, n)


def conv_pairs(x, w, first, rows, stride, n):
    parts = [jnp.concatenate([x[(first + q + j - 1) * stride : (first + q + j) * stride, :] for q in range(0, rows, 2)], axis=0)
             for j in range(4)]
    z = jnp.dot(jnp.concatenate(parts, axis=1), w[...], preferred_element_type=F32)
    return row_shifts(z, stride, 2 * n)


def body_kernel(axes, counts, shapes, *refs):
    (relu33, target33, relu32, relu31, relu22, target22, relu21,
     pool1, pool2, lin2, lin3, k21, k22, k31, k32, k33, x21, w21, twice) = refs[:19]
    scratch = refs[19:]
    inputs = (None, relu32, relu31, relu22, target22, relu21)
    p33, t33 = scratch[:2]
    bufs = (None,) + tuple(scratch[2:7])
    sides, side_in, corner_in = scratch[7:13], scratch[13:19], scratch[19:25]
    (x33, x32, x31, x22, w33, w32, w31, w22, k21v, lin2v, lin3v, p1, p2, pedge, prow, pcol, pcor, upy, upp, injs,
     own_sem, w_sem, pair_sem, misc_sem, seed_send, seed_recv, send_sem, recv_sem) = scratch[25:]
    n = 6
    off = [OFF3, OFF3, OFF3, OFF2, OFF2, OFF2]
    h3, wd3, c3 = shapes[0]
    h2, wd2, c2 = shapes[3]
    s3, s2 = wd3 + 2 * SIDE, wd2 + 2 * SIDE

    def own(a):
        return pltpu.make_async_copy(
            inputs[a], bufs[a].at[off[a] : off[a] + shapes[a][0], 0 : shapes[a][1]], own_sem.at[a])

    def weights(i):
        if i == 3:
            return [pltpu.make_async_copy(
                k22.at[:, tap * c2 : (tap + 1) * c2],
                w22.at[(p + 2 - tap // 3) * c2 : (p + 3 - tap // 3) * c2, (2 * (tap % 3) + p) * c2 : (2 * (tap % 3) + p + 1) * c2],
                pair_sem.at[p, tap]) for p in range(2) for tap in range(9)]
        k, w = ((k33, w33), (k32, w32), (k31, w31))[i]
        o, cols = k.shape[0], k.shape[1] // 3
        return [pltpu.make_async_copy(k.at[:, dy * cols : (dy + 1) * cols], w.at[dy * o : (dy + 1) * o], w_sem.at[i, dy])
                for dy in range(3)]

    others = [pltpu.make_async_copy(src, dst, misc_sem.at[i])
              for i, (src, dst) in enumerate(((relu33, p33), (target33, t33), (pool2, p2), (pool1, p1), (k21, k21v), (lin3, lin3v), (lin2, lin2v)))]
    others[0].start()
    others[1].start()
    others[5].start()
    others[6].start()
    for a in (1, 2, 3, 4, 5):
        own(a).start()
    others[2].start()
    for i in range(4):
        for c in weights(i):
            c.start()
    others[4].start()
    others[3].start()

    me = tuple(lax.axis_index(axis) for axis in axes)

    def peer(d):
        return (me[0] + d[0], me[1] + d[1])

    barrier = pltpu.get_barrier_semaphore()
    for d in DIRS:
        @pl.when(reachable(axes, counts, d, 1))
        def _():
            pl.semaphore_signal(barrier, inc=1, device_id=peer(d), device_id_type=MESH)
    spans = [1 + jnp.minimum(m, 1) + jnp.minimum(c - 1 - m, 1) for m, c in zip(me, counts)]
    pl.semaphore_wait(barrier, spans[0] * spans[1] - 1)

    def remote(src, dst, ssem, rsem, d):
        return pltpu.make_async_remote_copy(
            src_ref=src, dst_ref=dst, send_sem=ssem, recv_sem=rsem, device_id=peer(d), device_id_type=MESH)

    def corner_tiles(a):
        k = SIDE // WIDTHS[a]
        return -(-ROWS[a] // k)

    def messages(a, k):
        d = DIRS[k]
        ssem, rsem = send_sem.at[a, k], recv_sem.at[a, k]
        if a == n:
            if d[1] == 0:
                return [remote(pedge.at[k], prow.at[k], ssem, rsem, d)]
            rows = {0: slice(0, h3), -1: slice(0, 8), 1: slice(h3 - 8, h3)}[d[0]]
            lanes = slice(0, 128) if d[1] < 0 else slice((wd3 - 1) * 128, wd3 * 128)
            dst = pcol.at[k - 2] if d[0] == 0 else pcor.at[k - 4]
            return [remote(pool2.at[rows, lanes], dst, ssem, rsem, d)]
        if d[1] == 0:
            h, rows = ROWS[a], shapes[a][0]
            first, land = (0, rows) if d[0] < 0 else (rows - h, -h)
            if a == 0:
                return [remote(x33.at[(OFF3 + first + q) * s3 : (OFF3 + first + q) * s3 + wd3],
                               x33.at[(OFF3 + land + q) * s3 : (OFF3 + land + q) * s3 + wd3],
                               seed_send.at[k, q], seed_recv.at[k, q], d) for q in range(h)]
            return [remote(inputs[a].at[first : first + h],
                           bufs[a].at[off[a] + land : off[a] + land + h, 0 : shapes[a][1]], ssem, rsem, d)]
        side = 0 if d[1] < 0 else 1
        if d[0] == 0:
            return [remote(sides[a].at[side], side_in[a].at[side], ssem, rsem, d)]
        tiles, total = corner_tiles(a), sides[a].shape[1]
        first = 0 if d[0] < 0 else total - tiles
        return [remote(sides[a].at[side, first : first + tiles], corner_in[a].at[k - 4], ssem, rsem, d)]

    def send(a, ks):
        for k in ks:
            @pl.when(reachable(axes, counts, DIRS[k], 1))
            def _():
                for c in messages(a, k):
                    c.start()

    def put(a, row, slot, tiles):
        count = tiles.shape[0]
        tiles = tiles.astype(BF16)
        if a == 0:
            for q in range(count):
                at = (OFF3 + row + q) * s3 + slot
                x33[at : at + SIDE, :] = tiles[q]
        else:
            bufs[a][off[a] + row : off[a] + row + count, slot : slot + SIDE, :] = tiles

    def receive(a):
        h, (rows, cols, c) = ROWS[a], shapes[a]
        for k in range(8):
            d = DIRS[k]
            first, count = {0: (0, rows), -1: (rows, h), 1: (-h, h)}[d[0]]
            side = 0 if d[1] < 0 else 1
            slot = cols if side == 0 else cols + SIDE

            @pl.when(reachable(axes, counts, d, -1))
            def _():
                for m in messages(a, k):
                    m.wait_recv()
                if d[1]:
                    tiles = side_in[a][side] if d[0] == 0 else corner_in[a][k - 4]
                    spread = unpacked(tiles.astype(F32), WIDTHS[a], side)
                    spread = spread[:count] if d[0] <= 0 else spread[spread.shape[0] - count :]
                    put(a, first, slot, spread)

            if a != 4:
                @pl.when(jnp.logical_not(reachable(axes, counts, d, -1)))
                def _():
                    if d[1]:
                        put(a, first, slot, jnp.zeros((count, SIDE, c), F32))
                    elif a == 0:
                        for q in range(count):
                            x33[(OFF3 + first + q) * s3 : (OFF3 + first + q) * s3 + wd3, :] = jnp.zeros((wd3, c), BF16)
                    else:
                        bufs[a][off[a] + first : off[a] + first + count, 0:cols, :] = jnp.zeros((count, cols, c), BF16)

    def pack(a, side):
        rows, cols, c = shapes[a]
        at = 0 if side == 0 else cols - SIDE
        if a == 0:
            tiles = jnp.stack([x33[(OFF3 + q) * s3 + at : (OFF3 + q) * s3 + at + SIDE, :] for q in range(rows)])
        else:
            tiles = bufs[a][off[a] : off[a] + rows, at : at + SIDE, :]
        sides[a][side] = packed(tiles.astype(F32), WIDTHS[a], side).astype(BF16)

    def send_all(a):
        send(a, (0, 1))
        own(a).wait()
        pack(a, 0)
        pack(a, 1)
        send(a, range(2, 8))

    send_all(1)
    others[0].wait()
    others[1].wait()
    others[5].wait()
    others[6].wait()
    weight3 = 2.0 * lin3v[...]
    weight2 = 2.0 * lin2v[...]
    def seed_rows(i):
        for q in range(2):
            p = p33[2 * i + q].astype(F32)
            t = t33[2 * i + q].astype(F32)
            seed = jnp.where(p > 0, injected(p, t, weight3), 0.0).astype(BF16)
            x33[pl.ds(pl.multiple_of((OFF3 + 2 * i + q) * s3, 16), wd3), :] = seed

    outer = ROWS[0] // 2

    @pl.loop(0, outer)
    def _(i):
        seed_rows(i)
        seed_rows(h3 // 2 - outer + i)

    send(0, (0, 1))

    @pl.loop(outer, h3 // 2 - outer)
    def _(i):
        seed_rows(i)

    pack(0, 0)
    pack(0, 1)
    send(0, range(2, 8))
    send_all(2)

    def masked_conv(x, w, p, y, first, rows, stride, channels):
        o = conv_rows(x, w, first, rows, stride, channels)
        pre = p[first : first + rows].astype(F32)
        y[first * stride : (first + rows) * stride, :] = jnp.where(pre > 0, o, 0.0).astype(BF16).reshape(rows * stride, channels)

    others[2].wait()
    for j in range(wd3):
        pedge[0, j : j + 1, :] = p2[0:1, j * 128 : (j + 1) * 128]
        pedge[1, j : j + 1, :] = p2[h3 - 1 : h3, j * 128 : (j + 1) * 128]
    for a in (3, 4):
        own(a).wait()

    for j in range(wd3):
        for i0 in range(0, h3, 8):
            blk = p2[i0 : i0 + 8, j * 128 : (j + 1) * 128]
            for b in range(2):
                upp[pl.ds((OFFU + i0) * s2 + 2 * j + b, 8, stride=s2), :] = blk
    others[4].wait()
    taps = [k21v[tap * 64 : (tap + 1) * 64, :].astype(F32) for tap in range(9)]
    for dy in range(3):
        for half, (p, q) in enumerate(((0, 2), (1, 1))):
            both = jnp.concatenate([taps[3 * dy + p], taps[3 * dy + q]], axis=0)
            w21[dy * c2 : (dy + 1) * c2, half * 128 : (half + 1) * 128] = both.T.astype(BF16)
    for dx in range(3):
        for p in range(2):
            w22[(3 - 3 * p) * c2 : (4 - 3 * p) * c2, (2 * dx + p) * c2 : (2 * dx + p + 1) * c2] = jnp.zeros((c2, c2), BF16)

    def inject_at(row, count, slot, width):
        p = bufs[3][pl.ds(row, count), slot : slot + width, :].reshape(count * width, c2).astype(F32)
        t = bufs[4][pl.ds(row, count), slot : slot + width, :].reshape(count * width, c2).astype(F32)
        value = injected(p, t, weight2)
        for q in range(count):
            injs[pl.ds(pl.multiple_of((row + q) * s2 + slot, 16), width), :] = value[q * width : (q + 1) * width]

    @pl.loop(0, h2 // 4)
    def _(i):
        inject_at(OFF2 + 4 * i, 4, 0, wd2)

    others[3].wait()

    @pl.loop(0, wd2 // 2)
    def _(g):
        blk = p1[:, pl.ds(pl.multiple_of(g * 128, 128), 128)]
        for a in range(2):
            twice[pl.ds(g * 2 * h2 + a, h2, stride=2), :] = blk

    send(n, range(8))
    for a in (3, 4, 5):
        send(a, (0, 1))
        if a == 5:
            own(a).wait()
        pack(a, 0)
        pack(a, 1)
        send(a, range(2, 8))
    receive(0)
    for c in weights(0):
        c.wait()
    receive(1)
    masked_conv(x33, w33, bufs[1], x32, OFF3 - 3, h3 + 6, s3, c3)
    receive(2)
    for c in weights(1):
        c.wait()
    masked_conv(x32, w32, bufs[2], x31, OFF3 - 2, h3 + 4, s3, c3)

    for k in range(8):
        @pl.when(reachable(axes, counts, DIRS[k], -1))
        def _():
            for m in messages(n, k):
                m.wait_recv()
    for b in range(2):
        upp[pl.ds((OFFU + h3) * s2 + b, wd3, stride=2), :] = prow[0]
        upp[pl.ds((OFFU - 1) * s2 + b, wd3, stride=2), :] = prow[1]
        for i0 in range(0, h3, 8):
            upp[pl.ds((OFFU + i0) * s2 + wd2 + b, 8, stride=s2), :] = pcol[0, i0 : i0 + 8]
            upp[pl.ds((OFFU + i0) * s2 + s2 - 2 + b, 8, stride=s2), :] = pcol[1, i0 : i0 + 8]
        upp[(OFFU + h3) * s2 + wd2 + b : (OFFU + h3) * s2 + wd2 + b + 1, :] = pcor[0, 0:1]
        upp[(OFFU + h3) * s2 + s2 - 2 + b : (OFFU + h3) * s2 + s2 - 2 + b + 1, :] = pcor[1, 0:1]
        upp[(OFFU - 1) * s2 + wd2 + b : (OFFU - 1) * s2 + wd2 + b + 1, :] = pcor[2, 7:8]
        upp[(OFFU - 1) * s2 + s2 - 2 + b : (OFFU - 1) * s2 + s2 - 2 + b + 1, :] = pcor[3, 7:8]

    receive(3)
    receive(4)
    for c in weights(2):
        c.wait()
    o = conv_rows(x31, w31, OFF3 - 1, h3 + 2, s3, c2)
    for q in range(h3 + 2):
        base = (OFFU - 1 + q) * s2
        for b in range(2):
            upy[pl.ds(base + b, wd3, stride=2), :] = o[q, :wd3]
            upy[pl.ds(base + wd2 + b, 4, stride=2), :] = o[q, wd3 : wd3 + 4]
            upy[pl.ds(base + s2 - 8 + b, 4, stride=2), :] = o[q, s3 - 4 :]

    for q in range(0, h2 + 4, SIDE):
        inject_at(OFF2 - 2 + q, min(SIDE, h2 + 4 - q), wd2, 2 * SIDE)
    inject_at(OFF2 - 2, 2, 0, wd2)
    inject_at(OFF2 + h2, 2, 0, wd2)
    par = lax.broadcasted_iota(jnp.int32, (s2, 128), 0) % 2

    @pl.loop(0, (h2 + 4) // 2)
    def _(half):
        at = pl.ds(pl.multiple_of((half + OFFU - 1) * s2, 16), s2)
        y = upy[at, :]
        m = upp[at, :]
        for i in range(2):
            row = OFF2 - 2 + 2 * half + i
            here = pl.ds(pl.multiple_of(row * s2, 16), s2)
            p = bufs[3][row].astype(F32)
            arriving = jnp.where(m == par + 2 * i, y, 0.0) + injs[here, :]
            x22[here, :] = jnp.where(p > 0, arriving, 0.0).astype(BF16)

    receive(5)
    for c in weights(3):
        c.wait()
    first, rows = OFF2 - 1, h2 + 2
    o = conv_pairs(x22, w22, first, rows, s2, c2)
    for q in range(rows):
        pre = bufs[5][first + q].astype(F32)
        half = o[q // 2, :, (q % 2) * c2 : (q % 2 + 1) * c2]
        x21[(first + q) * s2 : (first + q + 1) * s2, :] = jnp.where(pre > 0, half, 0.0).astype(BF16)

    for a in range(n + 1):
        for k in range(8):
            @pl.when(reachable(axes, counts, DIRS[k], 1))
            def _():
                for m in messages(a, k):
                    m.wait_send()


def tail_kernel(h2, wd2, c2, x21, w21, twice, out, yt, res, out_sem):
    s2 = wd2 + 2 * SIDE
    rows = 8
    low = lax.broadcasted_iota(jnp.int32, (rows, wd2, 128), 2) < 64
    lane_low = lax.broadcasted_iota(jnp.int32, (2 * rows, 128), 1) < 64
    want = (lax.broadcasted_iota(jnp.int32, (2 * rows, 128), 0) % 2) * 2 + jnp.where(lane_low, 0, 1)
    parts = []

    def conv(i):
        first = OFF2 + i * rows
        lhs = [x21[(first + 1 - dy) * s2 : (first + 1 - dy + rows) * s2, :] for dy in range(3)]
        z = jnp.dot(jnp.concatenate(lhs, axis=1), w21[...], preferred_element_type=F32).reshape(rows, s2, 256)
        sides = z[:, :, :128]
        t = jnp.where(low, pltpu.roll(sides, s2 - 1, 1)[:, :wd2], pltpu.roll(sides, 1, 1)[:, :wd2])
        y = t + pltpu.roll(t, 64, 2) + z[:, :wd2, 128:]
        for q in range(rows):
            for j0 in range(0, wd2, 8):
                for a in range(2):
                    yt[i, pl.ds(j0 * PITCH + 2 * q + a, 8, stride=PITCH), :] = y[q, j0 : j0 + 8]

    def select(i):
        here = slice(i * 2 * rows, (i + 1) * 2 * rows)
        for g in range(wd2 // 2):
            m = twice[g * 2 * h2 + i * 2 * rows : g * 2 * h2 + (i + 1) * 2 * rows, :]
            turned = pltpu.roll(m, 64, 1)
            for e in range(2):
                y = yt[i, (2 * g + e) * PITCH : (2 * g + e) * PITCH + 2 * rows, :]
                sel = jnp.where(lane_low, m, turned) if e == 0 else jnp.where(lane_low, turned, m)
                res[here, (2 * g + e) * 128 : (2 * g + e + 1) * 128] = jnp.where(sel == want, y, 0.0).astype(BF16)
        parts.append(pltpu.make_async_copy(res.at[here], out.at[here], out_sem.at[i]))
        parts[-1].start()

    steps = h2 // rows
    conv(0)
    for i in range(steps):
        if i + 1 < steps:
            conv(i + 1)
        select(i)
    for c in parts:
        c.wait()


def shards(axes, counts, relu21, relu22, relu31, relu32, relu33, target22, target33, pool1, pool2, lin2, lin3,
           k21, k22, k31, k32, k33):
    tensors = (relu33, target33, relu32, relu31, relu22, target22, relu21)
    shapes = tuple(t.shape for t in (relu33, relu32, relu31, relu22, target22, relu21))
    h3, wd3, c3 = relu33.shape
    h2, wd2, c2 = relu22.shape
    s3, s2 = wd3 + 2 * SIDE, wd2 + 2 * SIDE
    anywhere = pl.BlockSpec(memory_space=pltpu.HBM)
    vmem = pl.BlockSpec(memory_space=pltpu.VMEM)
    rows3, rows2 = h3 + 2 * OFF3, h2 + 2 * OFF2
    per = [SIDE // w for w in WIDTHS]
    scratch = [pltpu.VMEM((h3, wd3, c3), BF16)] * 2
    scratch += [pltpu.VMEM((rows3, s3, c3), BF16)] * 2 + [pltpu.VMEM((rows2, s2, c2), BF16)] * 3
    scratch += [pltpu.VMEM((2, s[0] // k, SIDE, s[2]), BF16) for s, k in zip(shapes, per)] * 2
    scratch += [pltpu.VMEM((4, -(-r // k), SIDE, s[2]), BF16) for s, k, r in zip(shapes, per, ROWS)]
    scratch += [pltpu.VMEM((rows3 * s3, c3), BF16)] * 3 + [pltpu.VMEM((rows2 * s2, c2), BF16)]
    scratch += [pltpu.VMEM((3 * k.shape[0], k.shape[1] // 3), BF16) for k in (k33, k32, k31)]
    scratch += [
        pltpu.VMEM((4 * c2, 6 * c2), BF16),
        pltpu.VMEM(k21.shape[::-1], BF16),
        pltpu.VMEM((1, c2), F32),
        pltpu.VMEM((1, c3), F32),
        pltpu.VMEM(pool1.shape, jnp.int32),
        pltpu.VMEM(pool2.shape, jnp.int32),
        pltpu.VMEM((2, wd3, 128), jnp.int32),
        pltpu.VMEM((2, wd3, 128), jnp.int32),
        pltpu.VMEM((2, h3, 128), jnp.int32),
        pltpu.VMEM((4, 8, 128), jnp.int32),
        pltpu.VMEM(((h3 + 2 * OFFU + 1) * s2, 128), F32),
        pltpu.VMEM(((h3 + 2 * OFFU + 1) * s2, 128), jnp.int32),
        pltpu.VMEM((rows2 * s2, c2), F32),
        pltpu.SemaphoreType.DMA((6,)),
        pltpu.SemaphoreType.DMA((3, 3)),
        pltpu.SemaphoreType.DMA((2, 9)),
        pltpu.SemaphoreType.DMA((7,)),
        pltpu.SemaphoreType.DMA((2, 4)),
        pltpu.SemaphoreType.DMA((2, 4)),
        pltpu.SemaphoreType.DMA((7, 8)),
        pltpu.SemaphoreType.DMA((7, 8)),
    ]
    x21, w21, twice = pl.pallas_call(
        functools.partial(body_kernel, axes, counts, shapes),
        out_shape=[pltpu.VMEM((rows2 * s2, c2), BF16), pltpu.VMEM((3 * c2, 256), BF16), pltpu.VMEM((wd2 * h2, 128), jnp.int32)],
        in_specs=[anywhere] * 16,
        out_specs=[vmem] * 3,
        scratch_shapes=scratch,
        compiler_params=pltpu.CompilerParams(
            vmem_limit_bytes=40 * 1024 * 1024, collective_id=0, has_side_effects=True),
        name="body",
    )(*(pltpu.with_memory_space_constraint(v, pltpu.HBM) for v in (*tensors, pool1, pool2, lin2.reshape(1, c2), lin3.reshape(1, c3),
                                                                       k21.T, k22, k31, k32, k33)))
    return pl.pallas_call(
        functools.partial(tail_kernel, h2, wd2, c2),
        out_shape=jax.ShapeDtypeStruct((2 * h2, wd2 * 128), BF16),
        in_specs=[vmem] * 3,
        out_specs=anywhere,
        scratch_shapes=[
            pltpu.VMEM((h2 // 8, wd2 * PITCH + 8, 128), F32),
            pltpu.VMEM((2 * h2, wd2 * 128), BF16),
            pltpu.SemaphoreType.DMA((h2 // 8,)),
        ],
        compiler_params=pltpu.CompilerParams(vmem_limit_bytes=16 * 1024 * 1024),
        name="tail",
    )(*(pltpu.with_memory_space_constraint(v, pltpu.VMEM) for v in (x21, w21, twice)))


def solution(mesh):
    axes = ("row", "col")
    counts = tuple(mesh.shape[a] for a in axes)
    cells = P("row", "col", None)
    in_specs = (cells,) * 7 + (P("row", "col"),) * 2 + (P(),) * 7
    return jax.shard_map(functools.partial(shards, axes, counts), mesh=mesh, in_specs=in_specs,
                         out_specs=P("row", "col"), check_vma=False)
```

```python
import functools

import jax
import jax.numpy as jnp
from jax import lax
from jax.experimental import pallas as pl
from jax.experimental.pallas import tpu as pltpu
from jax.sharding import PartitionSpec as P

EPSILON = 1e-06
MESH = pl.DeviceIdType.MESH
F32 = jnp.float32
BF16 = jnp.bfloat16
SIDE = 8
OFF3 = 6
OFF2 = 4
OFFU = 2
SEED_ROWS = 4
PITCH = 17
DIRS = ((-1, 0), (1, 0), (0, -1), (0, 1), (-1, -1), (-1, 1), (1, -1), (1, 1))


WIDTHS = (4, 4, 2, 2, 2, 1)
ROWS = (4, 3, 2, 2, 2, 1)


def reachable(axes, counts, d, sign):
    checks = []
    for axis, count, step in zip(axes, counts, d):
        if step:
            target = lax.axis_index(axis) + sign * step
            checks.append(target >= 0 if sign * step < 0 else target < count)
    ok = checks[0]
    for c in checks[1:]:
        ok = jnp.logical_and(ok, c)
    return ok


def packed(tiles, width, side):
    k = SIDE // width
    rows, _, c = tiles.shape
    grouped = tiles.reshape(rows // k, k, SIDE, c)
    sub = lax.broadcasted_iota(jnp.int32, (rows // k, SIDE, c), 1)
    total = None
    for i in range(k):
        shift = (i * width - (0 if side == 0 else SIDE - width)) % SIDE
        piece = grouped[:, i]
        if shift:
            piece = pltpu.roll(piece, shift, 1)
        total = piece if total is None else jnp.where(sub >= i * width, piece, total)
    return total


def unpacked(tiles, width, side):
    k = SIDE // width
    count, _, c = tiles.shape
    pieces = []
    for i in range(k):
        shift = ((0 if side == 0 else SIDE - width) - i * width) % SIDE
        pieces.append(pltpu.roll(tiles, shift, 1) if shift else tiles)
    return jnp.stack(pieces, axis=1).reshape(count * k, SIDE, c)


def injected(p, t, weight):
    n = p.shape[-1]
    f = jnp.maximum(p, 0.0)
    g = jnp.maximum(t, 0.0)
    wf = weight * f
    ff = jnp.sum(f * f, axis=-1, keepdims=True)
    gg = jnp.sum(g * g, axis=-1, keepdims=True)
    wff = jnp.sum(wf * f, axis=-1, keepdims=True)
    wfg = jnp.sum(wf * g, axis=-1, keepdims=True)
    rinv = lax.rsqrt(ff * (1.0 / n) + EPSILON)
    both = rinv * lax.rsqrt(gg * (1.0 / n) + EPSILON)
    own = rinv * rinv
    level = (own * wff - both * wfg) * (1.0 / n)
    return own * (wf - level * f) - both * (weight * g)


def row_shifts(z, stride, n):
    z = z.reshape(-1, stride, 3 * n)
    return pltpu.roll(z[:, :, :n], stride - 1, 1) + z[:, :, n : 2 * n] + pltpu.roll(z[:, :, 2 * n :], 1, 1)


def conv_rows(x, w, first, rows, stride, n):
    half = rows // 2
    def part(at):
        parts = [x[(at + 1 - dy) * stride : (at + 1 - dy + half) * stride, :] for dy in range(3)]
        z = jnp.dot(jnp.concatenate(parts, axis=1), w[...], preferred_element_type=F32)
        return row_shifts(z, stride, n)
    return jnp.concatenate([part(first), part(first + half)], axis=0)


def conv_pairs(x, w, first, rows, stride, n):
    def part(at, count):
        parts = [jnp.concatenate([x[(at + q + j - 1) * stride : (at + q + j) * stride, :] for q in range(0, count, 2)], axis=0)
                 for j in range(4)]
        z = jnp.dot(jnp.concatenate(parts, axis=1), w[...], preferred_element_type=F32)
        return row_shifts(z, stride, 2 * n)

    half = rows // 4 * 2
    return jnp.concatenate([part(first, half), part(first + half, rows - half)], axis=0)


def body_kernel(axes, counts, shapes, *refs):
    (relu33, target33, relu32, relu31, relu22, target22, relu21,
     pool1, pool2, lin2, lin3, k21, k22, k31, k32, k33, x21, w21, twice) = refs[:19]
    scratch = refs[19:]
    inputs = (None, relu32, relu31, relu22, target22, relu21)
    p33, t33 = scratch[:2]
    bufs = (None,) + tuple(scratch[2:7])
    sides, side_in, corner_in = scratch[7:13], scratch[13:19], scratch[19:25]
    (x33, x32, x31, x22, w33, w32, w31, w22, k21v, lin2v, lin3v, p1, p2, pedge, prow, pcol, pcor, upy, upp, injs,
     own_sem, w_sem, pair_sem, misc_sem, send_sem, recv_sem) = scratch[25:]
    n = 6
    off = [OFF3, OFF3, OFF3, OFF2, OFF2, OFF2]
    h3, wd3, c3 = shapes[0]
    h2, wd2, c2 = shapes[3]
    s3, s2 = wd3 + 2 * SIDE, wd2 + 2 * SIDE

    def own(a):
        return pltpu.make_async_copy(
            inputs[a], bufs[a].at[off[a] : off[a] + shapes[a][0], 0 : shapes[a][1]], own_sem.at[a])

    def weights(i):
        if i == 3:
            return [pltpu.make_async_copy(
                k22.at[:, tap * c2 : (tap + 1) * c2],
                w22.at[(p + 2 - tap // 3) * c2 : (p + 3 - tap // 3) * c2, (2 * (tap % 3) + p) * c2 : (2 * (tap % 3) + p + 1) * c2],
                pair_sem.at[p, tap]) for p in range(2) for tap in range(9)]
        k, w = ((k33, w33), (k32, w32), (k31, w31))[i]
        o, cols = k.shape[0], k.shape[1] // 3
        return [pltpu.make_async_copy(k.at[:, dy * cols : (dy + 1) * cols], w.at[dy * o : (dy + 1) * o], w_sem.at[i, dy])
                for dy in range(3)]

    others = [pltpu.make_async_copy(src, dst, misc_sem.at[i])
              for i, (src, dst) in enumerate(((relu33, p33), (target33, t33), (pool2, p2), (pool1, p1), (k21, k21v), (lin3, lin3v), (lin2, lin2v)))]
    others[0].start()
    others[1].start()
    others[5].start()
    others[6].start()
    for a in (1, 2, 3, 4, 5):
        own(a).start()
    others[2].start()
    for i in range(4):
        for c in weights(i):
            c.start()
    others[4].start()
    others[3].start()

    me = tuple(lax.axis_index(axis) for axis in axes)

    def peer(d):
        return (me[0] + d[0], me[1] + d[1])

    barrier = pltpu.get_barrier_semaphore()
    for d in DIRS:
        @pl.when(reachable(axes, counts, d, 1))
        def _():
            pl.semaphore_signal(barrier, inc=1, device_id=peer(d), device_id_type=MESH)
    spans = [1 + jnp.minimum(m, 1) + jnp.minimum(c - 1 - m, 1) for m, c in zip(me, counts)]
    pl.semaphore_wait(barrier, spans[0] * spans[1] - 1)

    def remote(src, dst, ssem, rsem, d):
        return pltpu.make_async_remote_copy(
            src_ref=src, dst_ref=dst, send_sem=ssem, recv_sem=rsem, device_id=peer(d), device_id_type=MESH)

    def corner_tiles(a):
        k = SIDE // WIDTHS[a]
        return -(-ROWS[a] // k)

    def messages(a, k):
        d = DIRS[k]
        ssem, rsem = send_sem.at[k], recv_sem.at[a, k]
        if a == n:
            if d[1] == 0:
                return [remote(pedge.at[k], prow.at[k], ssem, rsem, d)]
            rows = {0: slice(0, h3), -1: slice(0, 8), 1: slice(h3 - 8, h3)}[d[0]]
            lanes = slice(0, 128) if d[1] < 0 else slice((wd3 - 1) * 128, wd3 * 128)
            dst = pcol.at[k - 2] if d[0] == 0 else pcor.at[k - 4]
            return [remote(pool2.at[rows, lanes], dst, ssem, rsem, d)]
        if d[1] == 0:
            h, rows = ROWS[a], shapes[a][0]
            first, land = (0, rows) if d[0] < 0 else (rows - h, -h)
            if a == 0:
                seeds = x33.reshape(h3 + 2 * OFF3, s3, c3)
                return [remote(seeds.at[OFF3 + first : OFF3 + first + h, 0:wd3],
                               seeds.at[OFF3 + land : OFF3 + land + h, 0:wd3], ssem, rsem, d)]
            return [remote(inputs[a].at[first : first + h],
                           bufs[a].at[off[a] + land : off[a] + land + h, 0 : shapes[a][1]], ssem, rsem, d)]
        side = 0 if d[1] < 0 else 1
        if d[0] == 0:
            return [remote(sides[a].at[side], side_in[a].at[side], ssem, rsem, d)]
        tiles, total = corner_tiles(a), sides[a].shape[1]
        first = 0 if d[0] < 0 else total - tiles
        return [remote(sides[a].at[side, first : first + tiles], corner_in[a].at[k - 4], ssem, rsem, d)]

    def sent_bytes(k):
        d = DIRS[k]
        total = 4 * 128 * (wd3 if d[1] == 0 else h3 if d[0] == 0 else 8)
        for a, (_, cols, c) in enumerate(shapes):
            if d[1] == 0:
                total += 2 * ROWS[a] * cols * c
            else:
                total += 2 * SIDE * c * (sides[a].shape[1] if d[0] == 0 else corner_tiles(a))
        return total

    def send(a, ks):
        for k in ks:
            @pl.when(reachable(axes, counts, DIRS[k], 1))
            def _():
                for c in messages(a, k):
                    c.start()

    def put(a, row, slot, tiles):
        count = tiles.shape[0]
        tiles = tiles.astype(BF16)
        if a == 0:
            for q in range(count):
                at = (OFF3 + row + q) * s3 + slot
                x33[at : at + SIDE, :] = tiles[q]
        else:
            bufs[a][off[a] + row : off[a] + row + count, slot : slot + SIDE, :] = tiles

    def receive(a):
        h, (rows, cols, c) = ROWS[a], shapes[a]
        for k in range(8):
            d = DIRS[k]
            first, count = {0: (0, rows), -1: (rows, h), 1: (-h, h)}[d[0]]
            side = 0 if d[1] < 0 else 1
            slot = cols if side == 0 else cols + SIDE

            @pl.when(reachable(axes, counts, d, -1))
            def _():
                for m in messages(a, k):
                    m.wait_recv()
                if d[1]:
                    tiles = side_in[a][side] if d[0] == 0 else corner_in[a][k - 4]
                    spread = unpacked(tiles.astype(F32), WIDTHS[a], side)
                    spread = spread[:count] if d[0] <= 0 else spread[spread.shape[0] - count :]
                    put(a, first, slot, spread)

            if a != 4:
                @pl.when(jnp.logical_not(reachable(axes, counts, d, -1)))
                def _():
                    if d[1]:
                        put(a, first, slot, jnp.zeros((count, SIDE, c), F32))
                    elif a == 0:
                        for q in range(count):
                            x33[(OFF3 + first + q) * s3 : (OFF3 + first + q) * s3 + wd3, :] = jnp.zeros((wd3, c), BF16)
                    else:
                        bufs[a][off[a] + first : off[a] + first + count, 0:cols, :] = jnp.zeros((count, cols, c), BF16)

    def pack(a, side):
        rows, cols, c = shapes[a]
        at = 0 if side == 0 else cols - SIDE
        if a == 0:
            tiles = jnp.stack([x33[(OFF3 + q) * s3 + at : (OFF3 + q) * s3 + at + SIDE, :] for q in range(rows)])
        else:
            tiles = bufs[a][off[a] : off[a] + rows, at : at + SIDE, :]
        sides[a][side] = packed(tiles.astype(F32), WIDTHS[a], side).astype(BF16)

    def send_all(a):
        send(a, (0, 1))
        if a not in (3, 4):
            own(a).wait()
        pack(a, 0)
        pack(a, 1)
        send(a, range(2, 8))

    send_all(1)
    others[0].wait()
    others[1].wait()
    others[5].wait()
    others[6].wait()
    weight3 = 2.0 * lin3v[...]
    weight2 = 2.0 * lin2v[...]

    @pl.loop(0, h3 // SEED_ROWS)
    def _(i):
        for q in range(SEED_ROWS):
            p = p33[SEED_ROWS * i + q].astype(F32)
            t = t33[SEED_ROWS * i + q].astype(F32)
            seed = jnp.where(p > 0, injected(p, t, weight3), 0.0).astype(BF16)
            x33[pl.ds(pl.multiple_of((OFF3 + SEED_ROWS * i + q) * s3, 16), wd3), :] = seed

    send(0, (0, 1))
    pack(0, 0)
    pack(0, 1)
    send(0, range(2, 8))
    send_all(2)
    def masked_conv(x, w, p, y, first, rows, stride, channels):
        o = conv_rows(x, w, first, rows, stride, channels)
        pre = p[first : first + rows].astype(F32)
        y[first * stride : (first + rows) * stride, :] = jnp.where(pre > 0, o, 0.0).astype(BF16).reshape(rows * stride, channels)

    others[2].wait()
    for j in range(wd3):
        pedge[0, j : j + 1, :] = p2[0:1, j * 128 : (j + 1) * 128]
        pedge[1, j : j + 1, :] = p2[h3 - 1 : h3, j * 128 : (j + 1) * 128]
    for j in range(wd3):
        for i0 in range(0, h3, 8):
            blk = p2[i0 : i0 + 8, j * 128 : (j + 1) * 128]
            for b in range(2):
                upp[pl.ds((OFFU + i0) * s2 + 2 * j + b, 8, stride=s2), :] = blk
    others[4].wait()
    taps = [k21v[tap * 64 : (tap + 1) * 64, :].astype(F32) for tap in range(9)]
    for dy in range(3):
        for half, (p, q) in enumerate(((0, 2), (1, 1))):
            both = jnp.concatenate([taps[3 * dy + p], taps[3 * dy + q]], axis=0)
            w21[dy * c2 : (dy + 1) * c2, half * 128 : (half + 1) * 128] = both.T.astype(BF16)
    for dx in range(3):
        for p in range(2):
            w22[(3 - 3 * p) * c2 : (4 - 3 * p) * c2, (2 * dx + p) * c2 : (2 * dx + p + 1) * c2] = jnp.zeros((c2, c2), BF16)

    def inject_at(row, count, slot, width):
        p = bufs[3][pl.ds(row, count), slot : slot + width, :].reshape(count * width, c2).astype(F32)
        t = bufs[4][pl.ds(row, count), slot : slot + width, :].reshape(count * width, c2).astype(F32)
        value = injected(p, t, weight2)
        for q in range(count):
            injs[pl.ds(pl.multiple_of((row + q) * s2 + slot, 16), width), :] = value[q * width : (q + 1) * width]

    own(3).wait()
    own(4).wait()

    @pl.loop(0, h2 // 4)
    def _(i):
        inject_at(OFF2 + 4 * i, 4, 0, wd2)

    others[3].wait()

    @pl.loop(0, wd2 // 2)
    def _(g):
        blk = p1[:, pl.ds(pl.multiple_of(g * 128, 128), 128)]
        for a in range(2):
            twice[pl.ds(g * 2 * h2 + a, h2, stride=2), :] = blk

    send(n, range(8))
    for a in (3, 4, 5):
        send_all(a)
    receive(0)
    for c in weights(0):
        c.wait()
    receive(1)
    masked_conv(x33, w33, bufs[1], x32, OFF3 - 3, h3 + 6, s3, c3)
    receive(2)
    for c in weights(1):
        c.wait()
    masked_conv(x32, w32, bufs[2], x31, OFF3 - 2, h3 + 4, s3, c3)

    for k in range(8):
        @pl.when(reachable(axes, counts, DIRS[k], -1))
        def _():
            for m in messages(n, k):
                m.wait_recv()
    for b in range(2):
        upp[pl.ds((OFFU + h3) * s2 + b, wd3, stride=2), :] = prow[0]
        upp[pl.ds((OFFU - 1) * s2 + b, wd3, stride=2), :] = prow[1]
        for i0 in range(0, h3, 8):
            upp[pl.ds((OFFU + i0) * s2 + wd2 + b, 8, stride=s2), :] = pcol[0, i0 : i0 + 8]
            upp[pl.ds((OFFU + i0) * s2 + s2 - 2 + b, 8, stride=s2), :] = pcol[1, i0 : i0 + 8]
        upp[(OFFU + h3) * s2 + wd2 + b : (OFFU + h3) * s2 + wd2 + b + 1, :] = pcor[0, 0:1]
        upp[(OFFU + h3) * s2 + s2 - 2 + b : (OFFU + h3) * s2 + s2 - 2 + b + 1, :] = pcor[1, 0:1]
        upp[(OFFU - 1) * s2 + wd2 + b : (OFFU - 1) * s2 + wd2 + b + 1, :] = pcor[2, 7:8]
        upp[(OFFU - 1) * s2 + s2 - 2 + b : (OFFU - 1) * s2 + s2 - 2 + b + 1, :] = pcor[3, 7:8]

    receive(3)
    receive(4)
    for c in weights(2):
        c.wait()
    o = conv_rows(x31, w31, OFF3 - 1, h3 + 2, s3, c2)
    for q in range(h3 + 2):
        base = (OFFU - 1 + q) * s2
        for b in range(2):
            upy[pl.ds(base + b, wd3, stride=2), :] = o[q, :wd3]
            upy[pl.ds(base + wd2 + b, 4, stride=2), :] = o[q, wd3 : wd3 + 4]
            upy[pl.ds(base + s2 - 8 + b, 4, stride=2), :] = o[q, s3 - 4 :]

    for q in range(0, h2 + 4, SIDE):
        inject_at(OFF2 - 2 + q, min(SIDE, h2 + 4 - q), wd2, 2 * SIDE)
    inject_at(OFF2 - 2, 2, 0, wd2)
    inject_at(OFF2 + h2, 2, 0, wd2)
    par = lax.broadcasted_iota(jnp.int32, (s2, 128), 0) % 2

    @pl.loop(0, (h2 + 4) // 2)
    def _(half):
        at = pl.ds(pl.multiple_of((half + OFFU - 1) * s2, 16), s2)
        y = upy[at, :]
        m = upp[at, :]
        for i in range(2):
            row = OFF2 - 2 + 2 * half + i
            here = pl.ds(pl.multiple_of(row * s2, 16), s2)
            p = bufs[3][row].astype(F32)
            arriving = jnp.where(m == par + 2 * i, y, 0.0) + injs[here, :]
            x22[here, :] = jnp.where(p > 0, arriving, 0.0).astype(BF16)

    receive(5)
    for c in weights(3):
        c.wait()
    first, rows = OFF2 - 1, h2 + 2
    o = conv_pairs(x22, w22, first, rows, s2, c2)
    for q in range(rows):
        pre = bufs[5][first + q].astype(F32)
        half = o[q // 2, :, (q % 2) * c2 : (q % 2 + 1) * c2]
        x21[(first + q) * s2 : (first + q + 1) * s2, :] = jnp.where(pre > 0, half, 0.0).astype(BF16)

    for k in range(8):
        @pl.when(reachable(axes, counts, DIRS[k], 1))
        def _():
            held = upy.at[0 : sent_bytes(k) // 512]
            remote(held, held, send_sem.at[k], recv_sem.at[0, k], DIRS[k]).wait_send()


def tail_kernel(h2, wd2, c2, x21, w21, twice, out, yt, res, out_sem):
    s2 = wd2 + 2 * SIDE
    rows = 8
    low = lax.broadcasted_iota(jnp.int32, (rows, wd2, 128), 2) < 64
    lane_low = lax.broadcasted_iota(jnp.int32, (2 * rows, 128), 1) < 64
    want = (lax.broadcasted_iota(jnp.int32, (2 * rows, 128), 0) % 2) * 2 + jnp.where(lane_low, 0, 1)
    parts = []

    def conv(i):
        first = OFF2 + i * rows
        lhs = [x21[(first + 1 - dy) * s2 : (first + 1 - dy + rows) * s2, :] for dy in range(3)]
        z = jnp.dot(jnp.concatenate(lhs, axis=1), w21[...], preferred_element_type=F32).reshape(rows, s2, 256)
        sides = z[:, :, :128]
        t = jnp.where(low, pltpu.roll(sides, s2 - 1, 1)[:, :wd2], pltpu.roll(sides, 1, 1)[:, :wd2])
        y = t + pltpu.roll(t, 64, 2) + z[:, :wd2, 128:]
        for q in range(rows):
            for j0 in range(0, wd2, 8):
                for a in range(2):
                    yt[i, pl.ds(j0 * PITCH + 2 * q + a, 8, stride=PITCH), :] = y[q, j0 : j0 + 8]

    def select(i):
        here = slice(i * 2 * rows, (i + 1) * 2 * rows)
        for g in range(wd2 // 2):
            m = twice[g * 2 * h2 + i * 2 * rows : g * 2 * h2 + (i + 1) * 2 * rows, :]
            turned = pltpu.roll(m, 64, 1)
            for e in range(2):
                y = yt[i, (2 * g + e) * PITCH : (2 * g + e) * PITCH + 2 * rows, :]
                sel = jnp.where(lane_low, m, turned) if e == 0 else jnp.where(lane_low, turned, m)
                res[here, (2 * g + e) * 128 : (2 * g + e + 1) * 128] = jnp.where(sel == want, y, 0.0).astype(BF16)
        parts.append(pltpu.make_async_copy(res.at[here], out.at[here], out_sem.at[i]))
        parts[-1].start()

    steps = h2 // rows
    conv(0)
    for i in range(steps):
        if i + 1 < steps:
            conv(i + 1)
        select(i)
    for c in parts:
        c.wait()


def shards(axes, counts, relu21, relu22, relu31, relu32, relu33, target22, target33, pool1, pool2, lin2, lin3,
           k21, k22, k31, k32, k33):
    tensors = (relu33, target33, relu32, relu31, relu22, target22, relu21)
    shapes = tuple(t.shape for t in (relu33, relu32, relu31, relu22, target22, relu21))
    h3, wd3, c3 = relu33.shape
    h2, wd2, c2 = relu22.shape
    s3, s2 = wd3 + 2 * SIDE, wd2 + 2 * SIDE
    anywhere = pl.BlockSpec(memory_space=pltpu.HBM)
    vmem = pl.BlockSpec(memory_space=pltpu.VMEM)
    rows3, rows2 = h3 + 2 * OFF3, h2 + 2 * OFF2
    per = [SIDE // w for w in WIDTHS]
    scratch = [pltpu.VMEM((h3, wd3, c3), BF16)] * 2
    scratch += [pltpu.VMEM((rows3, s3, c3), BF16)] * 2 + [pltpu.VMEM((rows2, s2, c2), BF16)] * 3
    scratch += [pltpu.VMEM((2, s[0] // k, SIDE, s[2]), BF16) for s, k in zip(shapes, per)] * 2
    scratch += [pltpu.VMEM((4, -(-r // k), SIDE, s[2]), BF16) for s, k, r in zip(shapes, per, ROWS)]
    scratch += [pltpu.VMEM((rows3 * s3, c3), BF16)] * 3 + [pltpu.VMEM((rows2 * s2, c2), BF16)]
    scratch += [pltpu.VMEM((3 * k.shape[0], k.shape[1] // 3), BF16) for k in (k33, k32, k31)]
    scratch += [
        pltpu.VMEM((4 * c2, 6 * c2), BF16),
        pltpu.VMEM(k21.shape[::-1], BF16),
        pltpu.VMEM((1, c2), F32),
        pltpu.VMEM((1, c3), F32),
        pltpu.VMEM(pool1.shape, jnp.int32),
        pltpu.VMEM(pool2.shape, jnp.int32),
        pltpu.VMEM((2, wd3, 128), jnp.int32),
        pltpu.VMEM((2, wd3, 128), jnp.int32),
        pltpu.VMEM((2, h3, 128), jnp.int32),
        pltpu.VMEM((4, 8, 128), jnp.int32),
        pltpu.VMEM(((h3 + 2 * OFFU + 1) * s2, 128), F32),
        pltpu.VMEM(((h3 + 2 * OFFU + 1) * s2, 128), jnp.int32),
        pltpu.VMEM((rows2 * s2, c2), F32),
        pltpu.SemaphoreType.DMA((6,)),
        pltpu.SemaphoreType.DMA((3, 3)),
        pltpu.SemaphoreType.DMA((2, 9)),
        pltpu.SemaphoreType.DMA((7,)),
        pltpu.SemaphoreType.DMA((8,)),
        pltpu.SemaphoreType.DMA((7, 8)),
    ]
    x21, w21, twice = pl.pallas_call(
        functools.partial(body_kernel, axes, counts, shapes),
        out_shape=[pltpu.VMEM((rows2 * s2, c2), BF16), pltpu.VMEM((3 * c2, 256), BF16), pltpu.VMEM((wd2 * h2, 128), jnp.int32)],
        in_specs=[anywhere] * 16,
        out_specs=[vmem] * 3,
        scratch_shapes=scratch,
        compiler_params=pltpu.CompilerParams(
            vmem_limit_bytes=40 * 1024 * 1024, collective_id=0, has_side_effects=True),
        name="body",
    )(*(pltpu.with_memory_space_constraint(v, pltpu.HBM) for v in (*tensors, pool1, pool2, lin2.reshape(1, c2), lin3.reshape(1, c3),
                                                                       k21.T, k22, k31, k32, k33)))
    return pl.pallas_call(
        functools.partial(tail_kernel, h2, wd2, c2),
        out_shape=jax.ShapeDtypeStruct((2 * h2, wd2 * 128), BF16),
        in_specs=[vmem] * 3,
        out_specs=anywhere,
        scratch_shapes=[
            pltpu.VMEM((h2 // 8, wd2 * PITCH + 8, 128), F32),
            pltpu.VMEM((2 * h2, wd2 * 128), BF16),
            pltpu.SemaphoreType.DMA((h2 // 8,)),
        ],
        compiler_params=pltpu.CompilerParams(vmem_limit_bytes=16 * 1024 * 1024),
        name="tail",
    )(*(pltpu.with_memory_space_constraint(v, pltpu.VMEM) for v in (x21, w21, twice)))


def solution(mesh):
    axes = ("row", "col")
    counts = tuple(mesh.shape[a] for a in axes)
    cells = P("row", "col", None)
    in_specs = (cells,) * 7 + (P("row", "col"),) * 2 + (P(),) * 7
    return jax.shard_map(functools.partial(shards, axes, counts), mesh=mesh, in_specs=in_specs,
                         out_specs=P("row", "col"), check_vma=False)
```

```python
import functools

import jax
import jax.numpy as jnp
from jax import lax
from jax.experimental import pallas as pl
from jax.experimental.pallas import tpu as pltpu
from jax.sharding import PartitionSpec as P

EPSILON = 1e-06
MESH = pl.DeviceIdType.MESH
F32 = jnp.float32
BF16 = jnp.bfloat16
SIDE = 8
OFF3 = 6
OFF2 = 4
OFFU = 2
SEED_ROWS = 4
PITCH = 17
DIRS = ((-1, 0), (1, 0), (0, -1), (0, 1), (-1, -1), (-1, 1), (1, -1), (1, 1))


WIDTHS = (4, 4, 2, 2, 2, 1)
ROWS = (4, 3, 2, 2, 2, 1)


def reachable(axes, counts, d, sign):
    checks = []
    for axis, count, step in zip(axes, counts, d):
        if step:
            target = lax.axis_index(axis) + sign * step
            checks.append(target >= 0 if sign * step < 0 else target < count)
    ok = checks[0]
    for c in checks[1:]:
        ok = jnp.logical_and(ok, c)
    return ok


def packed(tiles, width, side):
    k = SIDE // width
    rows, _, c = tiles.shape
    grouped = tiles.reshape(rows // k, k, SIDE, c)
    sub = lax.broadcasted_iota(jnp.int32, (rows // k, SIDE, c), 1)
    total = None
    for i in range(k):
        shift = (i * width - (0 if side == 0 else SIDE - width)) % SIDE
        piece = grouped[:, i]
        if shift:
            piece = pltpu.roll(piece, shift, 1)
        total = piece if total is None else jnp.where(sub >= i * width, piece, total)
    return total


def unpacked(tiles, width, side):
    k = SIDE // width
    count, _, c = tiles.shape
    pieces = []
    for i in range(k):
        shift = ((0 if side == 0 else SIDE - width) - i * width) % SIDE
        pieces.append(pltpu.roll(tiles, shift, 1) if shift else tiles)
    return jnp.stack(pieces, axis=1).reshape(count * k, SIDE, c)


def injected(p, t, weight):
    n = p.shape[-1]
    f = jnp.maximum(p, 0.0)
    g = jnp.maximum(t, 0.0)
    wf = weight * f
    ff = jnp.sum(f * f, axis=-1, keepdims=True)
    gg = jnp.sum(g * g, axis=-1, keepdims=True)
    wff = jnp.sum(wf * f, axis=-1, keepdims=True)
    wfg = jnp.sum(wf * g, axis=-1, keepdims=True)
    rinv = lax.rsqrt(ff * (1.0 / n) + EPSILON)
    both = rinv * lax.rsqrt(gg * (1.0 / n) + EPSILON)
    own = rinv * rinv
    level = (own * wff - both * wfg) * (1.0 / n)
    return own * (wf - level * f) - both * (weight * g)


def row_shifts(z, stride, n):
    z = z.reshape(-1, stride, 3 * n)
    return pltpu.roll(z[:, :, :n], stride - 1, 1) + z[:, :, n : 2 * n] + pltpu.roll(z[:, :, 2 * n :], 1, 1)


def conv_rows(x, w, first, rows, stride, n):
    half = rows // 2
    def part(at):
        parts = [x[(at + 1 - dy) * stride : (at + 1 - dy + half) * stride, :] for dy in range(3)]
        z = jnp.dot(jnp.concatenate(parts, axis=1), w[...], preferred_element_type=F32)
        return row_shifts(z, stride, n)
    return jnp.concatenate([part(first), part(first + half)], axis=0)


def conv_pairs(x, w, first, rows, stride, n):
    def part(at, count):
        parts = [jnp.concatenate([x[(at + q + j - 1) * stride : (at + q + j) * stride, :] for q in range(0, count, 2)], axis=0)
                 for j in range(4)]
        z = jnp.dot(jnp.concatenate(parts, axis=1), w[...], preferred_element_type=F32)
        return row_shifts(z, stride, 2 * n)

    half = rows // 4 * 2
    return jnp.concatenate([part(first, half), part(first + half, rows - half)], axis=0)


def body_kernel(axes, counts, shapes, *refs):
    (relu33, target33, relu32, relu31, relu22, target22, relu21,
     pool1, pool2, lin2, lin3, k21, k22, k31, k32, k33, x21, w21, twice) = refs[:19]
    scratch = refs[19:]
    inputs = (None, relu32, relu31, relu22, target22, relu21)
    p33, t33 = scratch[:2]
    bufs = (None,) + tuple(scratch[2:7])
    sides, side_in, corner_in = scratch[7:13], scratch[13:19], scratch[19:25]
    (x33, x32, x31, x22, w33, w32, w31, w22, k21v, lin2v, lin3v, p1, p2, pedge, prow, pcol, pcor, upy, upp, injs,
     own_sem, w_sem, pair_sem, misc_sem, send_sem, recv_sem) = scratch[25:]
    n = 6
    off = [OFF3, OFF3, OFF3, OFF2, OFF2, OFF2]
    h3, wd3, c3 = shapes[0]
    h2, wd2, c2 = shapes[3]
    s3, s2 = wd3 + 2 * SIDE, wd2 + 2 * SIDE

    def own(a):
        return pltpu.make_async_copy(
            inputs[a], bufs[a].at[off[a] : off[a] + shapes[a][0], 0 : shapes[a][1]], own_sem.at[a])

    def weights(i):
        if i == 3:
            return [pltpu.make_async_copy(
                k22.at[:, tap * c2 : (tap + 1) * c2],
                w22.at[(p + 2 - tap // 3) * c2 : (p + 3 - tap // 3) * c2, (2 * (tap % 3) + p) * c2 : (2 * (tap % 3) + p + 1) * c2],
                pair_sem.at[p, tap]) for p in range(2) for tap in range(9)]
        k, w = ((k33, w33), (k32, w32), (k31, w31))[i]
        o, cols = k.shape[0], k.shape[1] // 3
        return [pltpu.make_async_copy(k.at[:, dy * cols : (dy + 1) * cols], w.at[dy * o : (dy + 1) * o], w_sem.at[i, dy])
                for dy in range(3)]

    others = [pltpu.make_async_copy(src, dst, misc_sem.at[i])
              for i, (src, dst) in enumerate(((relu33, p33), (target33, t33), (pool2, p2), (pool1, p1), (k21, k21v), (lin3, lin3v), (lin2, lin2v)))]
    others[0].start()
    others[1].start()
    others[5].start()
    others[6].start()
    for a in (1, 2, 3, 4, 5):
        own(a).start()
    others[2].start()
    for i in range(4):
        for c in weights(i):
            c.start()
    others[4].start()
    others[3].start()

    me = tuple(lax.axis_index(axis) for axis in axes)

    def peer(d):
        return (me[0] + d[0], me[1] + d[1])

    barrier = pltpu.get_barrier_semaphore()
    for d in DIRS:
        @pl.when(reachable(axes, counts, d, 1))
        def _():
            pl.semaphore_signal(barrier, inc=1, device_id=peer(d), device_id_type=MESH)
    spans = [1 + jnp.minimum(m, 1) + jnp.minimum(c - 1 - m, 1) for m, c in zip(me, counts)]
    pl.semaphore_wait(barrier, spans[0] * spans[1] - 1)

    def remote(src, dst, ssem, rsem, d):
        return pltpu.make_async_remote_copy(
            src_ref=src, dst_ref=dst, send_sem=ssem, recv_sem=rsem, device_id=peer(d), device_id_type=MESH)

    def corner_tiles(a):
        k = SIDE // WIDTHS[a]
        return -(-ROWS[a] // k)

    def messages(a, k):
        d = DIRS[k]
        ssem, rsem = send_sem.at[k], recv_sem.at[a, k]
        if a == n:
            if d[1] == 0:
                return [remote(pedge.at[k], prow.at[k], ssem, rsem, d)]
            rows = {0: slice(0, h3), -1: slice(0, 8), 1: slice(h3 - 8, h3)}[d[0]]
            lanes = slice(0, 128) if d[1] < 0 else slice((wd3 - 1) * 128, wd3 * 128)
            dst = pcol.at[k - 2] if d[0] == 0 else pcor.at[k - 4]
            return [remote(pool2.at[rows, lanes], dst, ssem, rsem, d)]
        if d[1] == 0:
            h, rows = ROWS[a], shapes[a][0]
            first, land = (0, rows) if d[0] < 0 else (rows - h, -h)
            if a == 0:
                seeds = x33.reshape(h3 + 2 * OFF3, s3, c3)
                return [remote(seeds.at[OFF3 + first : OFF3 + first + h, 0:wd3],
                               seeds.at[OFF3 + land : OFF3 + land + h, 0:wd3], ssem, rsem, d)]
            return [remote(inputs[a].at[first : first + h],
                           bufs[a].at[off[a] + land : off[a] + land + h, 0 : shapes[a][1]], ssem, rsem, d)]
        side = 0 if d[1] < 0 else 1
        if d[0] == 0:
            return [remote(sides[a].at[side], side_in[a].at[side], ssem, rsem, d)]
        tiles, total = corner_tiles(a), sides[a].shape[1]
        first = 0 if d[0] < 0 else total - tiles
        return [remote(sides[a].at[side, first : first + tiles], corner_in[a].at[k - 4], ssem, rsem, d)]

    def sent_bytes(k):
        d = DIRS[k]
        total = 4 * 128 * (wd3 if d[1] == 0 else h3 if d[0] == 0 else 8)
        for a, (_, cols, c) in enumerate(shapes):
            if d[1] == 0:
                total += 2 * ROWS[a] * cols * c
            else:
                total += 2 * SIDE * c * (sides[a].shape[1] if d[0] == 0 else corner_tiles(a))
        return total

    def send(a, ks):
        for k in ks:
            @pl.when(reachable(axes, counts, DIRS[k], 1))
            def _():
                for c in messages(a, k):
                    c.start()

    def put(a, row, slot, tiles):
        count = tiles.shape[0]
        tiles = tiles.astype(BF16)
        if a == 0:
            for q in range(count):
                at = (OFF3 + row + q) * s3 + slot
                x33[at : at + SIDE, :] = tiles[q]
        else:
            bufs[a][off[a] + row : off[a] + row + count, slot : slot + SIDE, :] = tiles

    def receive(a):
        h, (rows, cols, c) = ROWS[a], shapes[a]
        for k in range(8):
            d = DIRS[k]
            first, count = {0: (0, rows), -1: (rows, h), 1: (-h, h)}[d[0]]
            side = 0 if d[1] < 0 else 1
            slot = cols if side == 0 else cols + SIDE

            @pl.when(reachable(axes, counts, d, -1))
            def _():
                for m in messages(a, k):
                    m.wait_recv()
                if d[1]:
                    tiles = side_in[a][side] if d[0] == 0 else corner_in[a][k - 4]
                    spread = unpacked(tiles.astype(F32), WIDTHS[a], side)
                    spread = spread[:count] if d[0] <= 0 else spread[spread.shape[0] - count :]
                    put(a, first, slot, spread)

            if a != 4:
                @pl.when(jnp.logical_not(reachable(axes, counts, d, -1)))
                def _():
                    if d[1]:
                        put(a, first, slot, jnp.zeros((count, SIDE, c), F32))
                    elif a == 0:
                        for q in range(count):
                            x33[(OFF3 + first + q) * s3 : (OFF3 + first + q) * s3 + wd3, :] = jnp.zeros((wd3, c), BF16)
                    else:
                        bufs[a][off[a] + first : off[a] + first + count, 0:cols, :] = jnp.zeros((count, cols, c), BF16)

    def pack(a, side):
        rows, cols, c = shapes[a]
        at = 0 if side == 0 else cols - SIDE
        if a == 0:
            tiles = jnp.stack([x33[(OFF3 + q) * s3 + at : (OFF3 + q) * s3 + at + SIDE, :] for q in range(rows)])
        else:
            tiles = bufs[a][off[a] : off[a] + rows, at : at + SIDE, :]
        sides[a][side] = packed(tiles.astype(F32), WIDTHS[a], side).astype(BF16)

    def send_all(a):
        send(a, (0, 1))
        if a not in (3, 4):
            own(a).wait()
        pack(a, 0)
        pack(a, 1)
        send(a, range(2, 8))

    send_all(1)
    others[0].wait()
    others[1].wait()
    others[5].wait()
    others[6].wait()
    weight3 = 2.0 * lin3v[...]
    weight2 = 2.0 * lin2v[...]

    for i in range(h3 // SEED_ROWS):
        for q in range(SEED_ROWS):
            p = p33[SEED_ROWS * i + q].astype(F32)
            t = t33[SEED_ROWS * i + q].astype(F32)
            seed = jnp.where(p > 0, injected(p, t, weight3), 0.0).astype(BF16)
            at = (OFF3 + SEED_ROWS * i + q) * s3
            x33[at : at + wd3, :] = seed

    pack(0, 0)
    pack(0, 1)
    send(0, (4, 5, 6, 7, 0, 1, 2, 3))
    send_all(2)
    def masked_conv(x, w, p, y, first, rows, stride, channels):
        o = conv_rows(x, w, first, rows, stride, channels)
        pre = p[first : first + rows].astype(F32)
        y[first * stride : (first + rows) * stride, :] = jnp.where(pre > 0, o, 0.0).astype(BF16).reshape(rows * stride, channels)

    others[2].wait()
    for j in range(wd3):
        pedge[0, j : j + 1, :] = p2[0:1, j * 128 : (j + 1) * 128]
        pedge[1, j : j + 1, :] = p2[h3 - 1 : h3, j * 128 : (j + 1) * 128]
    for j in range(wd3):
        for i0 in range(0, h3, 8):
            blk = p2[i0 : i0 + 8, j * 128 : (j + 1) * 128]
            for b in range(2):
                upp[pl.ds((OFFU + i0) * s2 + 2 * j + b, 8, stride=s2), :] = blk
    others[4].wait()
    taps = [k21v[tap * 64 : (tap + 1) * 64, :].astype(F32) for tap in range(9)]
    for dy in range(3):
        for half, (p, q) in enumerate(((0, 2), (1, 1))):
            both = jnp.concatenate([taps[3 * dy + p], taps[3 * dy + q]], axis=0)
            w21[dy * c2 : (dy + 1) * c2, half * 128 : (half + 1) * 128] = both.T.astype(BF16)
    for dx in range(3):
        for p in range(2):
            w22[(3 - 3 * p) * c2 : (4 - 3 * p) * c2, (2 * dx + p) * c2 : (2 * dx + p + 1) * c2] = jnp.zeros((c2, c2), BF16)

    def inject_at(row, count, slot, width):
        p = bufs[3][pl.ds(row, count), slot : slot + width, :].reshape(count * width, c2).astype(F32)
        t = bufs[4][pl.ds(row, count), slot : slot + width, :].reshape(count * width, c2).astype(F32)
        value = injected(p, t, weight2)
        for q in range(count):
            injs[pl.ds(pl.multiple_of((row + q) * s2 + slot, 16), width), :] = value[q * width : (q + 1) * width]

    own(3).wait()
    own(4).wait()

    @pl.loop(0, h2 // 4)
    def _(i):
        inject_at(OFF2 + 4 * i, 4, 0, wd2)

    others[3].wait()

    @pl.loop(0, wd2 // 2)
    def _(g):
        blk = p1[:, pl.ds(pl.multiple_of(g * 128, 128), 128)]
        for a in range(2):
            twice[pl.ds(g * 2 * h2 + a, h2, stride=2), :] = blk

    send(n, range(8))
    for a in (3, 4, 5):
        send_all(a)
    receive(0)
    for c in weights(0):
        c.wait()
    receive(1)
    masked_conv(x33, w33, bufs[1], x32, OFF3 - 3, h3 + 6, s3, c3)
    receive(2)
    for c in weights(1):
        c.wait()
    masked_conv(x32, w32, bufs[2], x31, OFF3 - 2, h3 + 4, s3, c3)

    for k in range(8):
        @pl.when(reachable(axes, counts, DIRS[k], -1))
        def _():
            for m in messages(n, k):
                m.wait_recv()
    for b in range(2):
        upp[pl.ds((OFFU + h3) * s2 + b, wd3, stride=2), :] = prow[0]
        upp[pl.ds((OFFU - 1) * s2 + b, wd3, stride=2), :] = prow[1]
        for i0 in range(0, h3, 8):
            upp[pl.ds((OFFU + i0) * s2 + wd2 + b, 8, stride=s2), :] = pcol[0, i0 : i0 + 8]
            upp[pl.ds((OFFU + i0) * s2 + s2 - 2 + b, 8, stride=s2), :] = pcol[1, i0 : i0 + 8]
        upp[(OFFU + h3) * s2 + wd2 + b : (OFFU + h3) * s2 + wd2 + b + 1, :] = pcor[0, 0:1]
        upp[(OFFU + h3) * s2 + s2 - 2 + b : (OFFU + h3) * s2 + s2 - 2 + b + 1, :] = pcor[1, 0:1]
        upp[(OFFU - 1) * s2 + wd2 + b : (OFFU - 1) * s2 + wd2 + b + 1, :] = pcor[2, 7:8]
        upp[(OFFU - 1) * s2 + s2 - 2 + b : (OFFU - 1) * s2 + s2 - 2 + b + 1, :] = pcor[3, 7:8]

    receive(3)
    receive(4)
    receive(5)
    for c in weights(3):
        c.wait()
    for c in weights(2):
        c.wait()
    o = conv_rows(x31, w31, OFF3 - 1, h3 + 2, s3, c2)
    for q in range(h3 + 2):
        base = (OFFU - 1 + q) * s2
        for b in range(2):
            upy[pl.ds(base + b, wd3, stride=2), :] = o[q, :wd3]
            upy[pl.ds(base + wd2 + b, 4, stride=2), :] = o[q, wd3 : wd3 + 4]
            upy[pl.ds(base + s2 - 8 + b, 4, stride=2), :] = o[q, s3 - 4 :]

    for q in range(0, h2 + 4, SIDE):
        inject_at(OFF2 - 2 + q, min(SIDE, h2 + 4 - q), wd2, 2 * SIDE)
    inject_at(OFF2 - 2, 2, 0, wd2)
    inject_at(OFF2 + h2, 2, 0, wd2)
    par = lax.broadcasted_iota(jnp.int32, (s2, 128), 0) % 2

    for half in range((h2 + 4) // 2):
        at = slice((half + OFFU - 1) * s2, (half + OFFU) * s2)
        y = upy[at, :]
        m = upp[at, :]
        for i in range(2):
            row = OFF2 - 2 + 2 * half + i
            here = slice(row * s2, (row + 1) * s2)
            p = bufs[3][row].astype(F32)
            arriving = jnp.where(m == par + 2 * i, y, 0.0) + injs[here, :]
            x22[here, :] = jnp.where(p > 0, arriving, 0.0).astype(BF16)

    first, rows = OFF2 - 1, h2 + 2
    o = conv_pairs(x22, w22, first, rows, s2, c2)
    for q in range(rows):
        pre = bufs[5][first + q].astype(F32)
        half = o[q // 2, :, (q % 2) * c2 : (q % 2 + 1) * c2]
        x21[(first + q) * s2 : (first + q + 1) * s2, :] = jnp.where(pre > 0, half, 0.0).astype(BF16)

    for k in range(8):
        @pl.when(reachable(axes, counts, DIRS[k], 1))
        def _():
            held = upy.at[0 : sent_bytes(k) // 512]
            remote(held, held, send_sem.at[k], recv_sem.at[0, k], DIRS[k]).wait_send()


def tail_kernel(h2, wd2, c2, x21, w21, twice, out, yt, res, out_sem):
    s2 = wd2 + 2 * SIDE
    rows = 8
    low = lax.broadcasted_iota(jnp.int32, (rows, wd2, 128), 2) < 64
    lane_low = lax.broadcasted_iota(jnp.int32, (2 * rows, 128), 1) < 64
    want = (lax.broadcasted_iota(jnp.int32, (2 * rows, 128), 0) % 2) * 2 + jnp.where(lane_low, 0, 1)
    parts = []

    def conv(i):
        first = OFF2 + i * rows
        lhs = [x21[(first + 1 - dy) * s2 : (first + 1 - dy + rows) * s2, :] for dy in range(3)]
        z = jnp.dot(jnp.concatenate(lhs, axis=1), w21[...], preferred_element_type=F32).reshape(rows, s2, 256)
        sides = z[:, :, :128]
        t = jnp.where(low, pltpu.roll(sides, s2 - 1, 1)[:, :wd2], pltpu.roll(sides, 1, 1)[:, :wd2])
        y = t + pltpu.roll(t, 64, 2) + z[:, :wd2, 128:]
        for q in range(rows):
            for j0 in range(0, wd2, 8):
                for a in range(2):
                    yt[i, pl.ds(j0 * PITCH + 2 * q + a, 8, stride=PITCH), :] = y[q, j0 : j0 + 8]

    def ship(i, here, side):
        lanes = slice(side * wd2 * 64, (side + 1) * wd2 * 64)
        parts.append(pltpu.make_async_copy(res.at[here, lanes], out.at[here, lanes], out_sem.at[i, side]))
        parts[-1].start()

    def select(i):
        here = slice(i * 2 * rows, (i + 1) * 2 * rows)
        for g in range(wd2 // 2):
            if g == wd2 // 4:
                ship(i, here, 0)
            m = twice[g * 2 * h2 + i * 2 * rows : g * 2 * h2 + (i + 1) * 2 * rows, :]
            turned = pltpu.roll(m, 64, 1)
            for e in range(2):
                y = yt[i, (2 * g + e) * PITCH : (2 * g + e) * PITCH + 2 * rows, :]
                sel = jnp.where(lane_low, m, turned) if e == 0 else jnp.where(lane_low, turned, m)
                res[here, (2 * g + e) * 128 : (2 * g + e + 1) * 128] = jnp.where(sel == want, y, 0.0).astype(BF16)
        ship(i, here, 1)

    steps = h2 // rows
    conv(0)
    for i in range(steps):
        if i + 1 < steps:
            conv(i + 1)
        select(i)
    for c in parts:
        c.wait()


def shards(axes, counts, relu21, relu22, relu31, relu32, relu33, target22, target33, pool1, pool2, lin2, lin3,
           k21, k22, k31, k32, k33):
    tensors = (relu33, target33, relu32, relu31, relu22, target22, relu21)
    shapes = tuple(t.shape for t in (relu33, relu32, relu31, relu22, target22, relu21))
    h3, wd3, c3 = relu33.shape
    h2, wd2, c2 = relu22.shape
    s3, s2 = wd3 + 2 * SIDE, wd2 + 2 * SIDE
    anywhere = pl.BlockSpec(memory_space=pltpu.HBM)
    vmem = pl.BlockSpec(memory_space=pltpu.VMEM)
    rows3, rows2 = h3 + 2 * OFF3, h2 + 2 * OFF2
    per = [SIDE // w for w in WIDTHS]
    scratch = [pltpu.VMEM((h3, wd3, c3), BF16)] * 2
    scratch += [pltpu.VMEM((rows3, s3, c3), BF16)] * 2 + [pltpu.VMEM((rows2, s2, c2), BF16)] * 3
    scratch += [pltpu.VMEM((2, s[0] // k, SIDE, s[2]), BF16) for s, k in zip(shapes, per)] * 2
    scratch += [pltpu.VMEM((4, -(-r // k), SIDE, s[2]), BF16) for s, k, r in zip(shapes, per, ROWS)]
    scratch += [pltpu.VMEM((rows3 * s3, c3), BF16)] * 3 + [pltpu.VMEM((rows2 * s2, c2), BF16)]
    scratch += [pltpu.VMEM((3 * k.shape[0], k.shape[1] // 3), BF16) for k in (k33, k32, k31)]
    scratch += [
        pltpu.VMEM((4 * c2, 6 * c2), BF16),
        pltpu.VMEM(k21.shape[::-1], BF16),
        pltpu.VMEM((1, c2), F32),
        pltpu.VMEM((1, c3), F32),
        pltpu.VMEM(pool1.shape, jnp.int32),
        pltpu.VMEM(pool2.shape, jnp.int32),
        pltpu.VMEM((2, wd3, 128), jnp.int32),
        pltpu.VMEM((2, wd3, 128), jnp.int32),
        pltpu.VMEM((2, h3, 128), jnp.int32),
        pltpu.VMEM((4, 8, 128), jnp.int32),
        pltpu.VMEM(((h3 + 2 * OFFU + 1) * s2, 128), F32),
        pltpu.VMEM(((h3 + 2 * OFFU + 1) * s2, 128), jnp.int32),
        pltpu.VMEM((rows2 * s2, c2), F32),
        pltpu.SemaphoreType.DMA((6,)),
        pltpu.SemaphoreType.DMA((3, 3)),
        pltpu.SemaphoreType.DMA((2, 9)),
        pltpu.SemaphoreType.DMA((7,)),
        pltpu.SemaphoreType.DMA((8,)),
        pltpu.SemaphoreType.DMA((7, 8)),
    ]
    x21, w21, twice = pl.pallas_call(
        functools.partial(body_kernel, axes, counts, shapes),
        out_shape=[pltpu.VMEM((rows2 * s2, c2), BF16), pltpu.VMEM((3 * c2, 256), BF16), pltpu.VMEM((wd2 * h2, 128), jnp.int32)],
        in_specs=[anywhere] * 16,
        out_specs=[vmem] * 3,
        scratch_shapes=scratch,
        compiler_params=pltpu.CompilerParams(
            vmem_limit_bytes=40 * 1024 * 1024, collective_id=0, has_side_effects=True),
        name="body",
    )(*(pltpu.with_memory_space_constraint(v, pltpu.HBM) for v in (*tensors, pool1, pool2, lin2.reshape(1, c2), lin3.reshape(1, c3),
                                                                       k21.T, k22, k31, k32, k33)))
    return pl.pallas_call(
        functools.partial(tail_kernel, h2, wd2, c2),
        out_shape=jax.ShapeDtypeStruct((2 * h2, wd2 * 128), BF16),
        in_specs=[vmem] * 3,
        out_specs=anywhere,
        scratch_shapes=[
            pltpu.VMEM((h2 // 8, wd2 * PITCH + 8, 128), F32),
            pltpu.VMEM((2 * h2, wd2 * 128), BF16),
            pltpu.SemaphoreType.DMA((h2 // 8, 2)),
        ],
        compiler_params=pltpu.CompilerParams(vmem_limit_bytes=16 * 1024 * 1024),
        name="tail",
    )(*(pltpu.with_memory_space_constraint(v, pltpu.VMEM) for v in (x21, w21, twice)))


def solution(mesh):
    axes = ("row", "col")
    counts = tuple(mesh.shape[a] for a in axes)
    cells = P("row", "col", None)
    in_specs = (cells,) * 7 + (P("row", "col"),) * 2 + (P(),) * 7
    return jax.shard_map(functools.partial(shards, axes, counts), mesh=mesh, in_specs=in_specs,
                         out_specs=P("row", "col"), check_vma=False)
```

```python
import functools

import jax
import jax.numpy as jnp
from jax import lax
from jax.experimental import pallas as pl
from jax.experimental.pallas import tpu as pltpu
from jax.sharding import PartitionSpec as P

EPSILON = 1e-06
MESH = pl.DeviceIdType.MESH
F32 = jnp.float32
BF16 = jnp.bfloat16
SIDE = 8
OFF3 = 6
OFF2 = 4
OFFU = 2
SEED_ROWS = 4
PITCH = 17
DIRS = ((-1, 0), (1, 0), (0, -1), (0, 1), (-1, -1), (-1, 1), (1, -1), (1, 1))


WIDTHS = (4, 4, 2, 2, 2, 1)
ROWS = (4, 3, 2, 2, 2, 1)


def reachable(axes, counts, d, sign):
    checks = []
    for axis, count, step in zip(axes, counts, d):
        if step:
            target = lax.axis_index(axis) + sign * step
            checks.append(target >= 0 if sign * step < 0 else target < count)
    ok = checks[0]
    for c in checks[1:]:
        ok = jnp.logical_and(ok, c)
    return ok


def packed(tiles, width, side):
    k = SIDE // width
    rows, _, c = tiles.shape
    grouped = tiles.reshape(rows // k, k, SIDE, c)
    sub = lax.broadcasted_iota(jnp.int32, (rows // k, SIDE, c), 1)
    total = None
    for i in range(k):
        shift = (i * width - (0 if side == 0 else SIDE - width)) % SIDE
        piece = grouped[:, i]
        if shift:
            piece = pltpu.roll(piece, shift, 1)
        total = piece if total is None else jnp.where(sub >= i * width, piece, total)
    return total


def unpacked(tiles, width, side):
    k = SIDE // width
    count, _, c = tiles.shape
    pieces = []
    for i in range(k):
        shift = ((0 if side == 0 else SIDE - width) - i * width) % SIDE
        pieces.append(pltpu.roll(tiles, shift, 1) if shift else tiles)
    return jnp.stack(pieces, axis=1).reshape(count * k, SIDE, c)


def injected(p, t, weight):
    n = p.shape[-1]
    f = jnp.maximum(p, 0.0)
    g = jnp.maximum(t, 0.0)
    wf = weight * f
    ff = jnp.sum(f * f, axis=-1, keepdims=True)
    gg = jnp.sum(g * g, axis=-1, keepdims=True)
    wff = jnp.sum(wf * f, axis=-1, keepdims=True)
    wfg = jnp.sum(wf * g, axis=-1, keepdims=True)
    rinv = lax.rsqrt(ff * (1.0 / n) + EPSILON)
    both = rinv * lax.rsqrt(gg * (1.0 / n) + EPSILON)
    own = rinv * rinv
    level = (own * wff - both * wfg) * (1.0 / n)
    return own * (wf - level * f) - both * (weight * g)


def row_shifts(z, stride, n):
    z = z.reshape(-1, stride, 3 * n)
    return pltpu.roll(z[:, :, :n], stride - 1, 1) + z[:, :, n : 2 * n] + pltpu.roll(z[:, :, 2 * n :], 1, 1)


def conv_rows(x, w, first, rows, stride, n):
    half = rows // 2
    def part(at):
        parts = [x[(at + 1 - dy) * stride : (at + 1 - dy + half) * stride, :] for dy in range(3)]
        z = jnp.dot(jnp.concatenate(parts, axis=1), w[...], preferred_element_type=F32)
        return row_shifts(z, stride, n)
    return jnp.concatenate([part(first), part(first + half)], axis=0)


def conv_pairs(x, w, first, rows, stride, n):
    def part(at, count):
        parts = [jnp.concatenate([x[(at + q + j - 1) * stride : (at + q + j) * stride, :] for q in range(0, count, 2)], axis=0)
                 for j in range(4)]
        z = jnp.dot(jnp.concatenate(parts, axis=1), w[...], preferred_element_type=F32)
        return row_shifts(z, stride, 2 * n)

    half = rows // 4 * 2
    return jnp.concatenate([part(first, half), part(first + half, rows - half)], axis=0)


def body_kernel(axes, counts, shapes, *refs):
    (relu33, target33, relu32, relu31, relu22, target22, relu21,
     pool1, pool2, lin2, lin3, k21, k22, k31, k32, k33, x21, w21, twice) = refs[:19]
    scratch = refs[19:]
    inputs = (None, relu32, relu31, relu22, target22, relu21)
    p33, t33 = scratch[:2]
    bufs = (None,) + tuple(scratch[2:7])
    sides, side_in, corner_in = scratch[7:13], scratch[13:19], scratch[19:25]
    (x33, x33t, x32, x31, x22, w33, w32, w31, w22, k21v, lin2v, lin3v, p1, p2, pedge, prow, pcol, pcor, upy, upp, injs,
     own_sem, w_sem, pair_sem, misc_sem, send_sem, recv_sem) = scratch[25:]
    n = 6
    off = [OFF3, OFF3, OFF3, OFF2, OFF2, OFF2]
    h3, wd3, c3 = shapes[0]
    h2, wd2, c2 = shapes[3]
    s3, s2 = wd3 + 2 * SIDE, wd2 + 2 * SIDE
    tight = wd3 + SIDE

    def own(a):
        return pltpu.make_async_copy(
            inputs[a], bufs[a].at[off[a] : off[a] + shapes[a][0], 0 : shapes[a][1]], own_sem.at[a])

    def weights(i):
        if i == 3:
            return [pltpu.make_async_copy(
                k22.at[:, tap * c2 : (tap + 1) * c2],
                w22.at[(p + 2 - tap // 3) * c2 : (p + 3 - tap // 3) * c2, (2 * (tap % 3) + p) * c2 : (2 * (tap % 3) + p + 1) * c2],
                pair_sem.at[p, tap]) for p in range(2) for tap in range(9)]
        k, w = ((k33, w33), (k32, w32), (k31, w31))[i]
        o, cols = k.shape[0], k.shape[1] // 3
        return [pltpu.make_async_copy(k.at[:, dy * cols : (dy + 1) * cols], w.at[dy * o : (dy + 1) * o], w_sem.at[i, dy])
                for dy in range(3)]

    others = [pltpu.make_async_copy(src, dst, misc_sem.at[i])
              for i, (src, dst) in enumerate(((relu33, p33), (target33, t33), (pool2, p2), (pool1, p1), (k21, k21v), (lin3, lin3v), (lin2, lin2v)))]
    others[0].start()
    others[1].start()
    others[5].start()
    others[6].start()
    for a in (1, 2, 3, 4, 5):
        own(a).start()
    others[2].start()
    for i in range(4):
        for c in weights(i):
            c.start()
    others[4].start()
    others[3].start()

    me = tuple(lax.axis_index(axis) for axis in axes)

    def peer(d):
        return (me[0] + d[0], me[1] + d[1])

    barrier = pltpu.get_barrier_semaphore()
    for d in DIRS:
        @pl.when(reachable(axes, counts, d, 1))
        def _():
            pl.semaphore_signal(barrier, inc=1, device_id=peer(d), device_id_type=MESH)
    spans = [1 + jnp.minimum(m, 1) + jnp.minimum(c - 1 - m, 1) for m, c in zip(me, counts)]
    pl.semaphore_wait(barrier, spans[0] * spans[1] - 1)

    def remote(src, dst, ssem, rsem, d):
        return pltpu.make_async_remote_copy(
            src_ref=src, dst_ref=dst, send_sem=ssem, recv_sem=rsem, device_id=peer(d), device_id_type=MESH)

    def corner_tiles(a):
        k = SIDE // WIDTHS[a]
        return -(-ROWS[a] // k)

    def messages(a, k):
        d = DIRS[k]
        ssem, rsem = send_sem.at[k], recv_sem.at[a, k]
        if a == n:
            if d[1] == 0:
                return [remote(pedge.at[k], prow.at[k], ssem, rsem, d)]
            rows = {0: slice(0, h3), -1: slice(0, 8), 1: slice(h3 - 8, h3)}[d[0]]
            lanes = slice(0, 128) if d[1] < 0 else slice((wd3 - 1) * 128, wd3 * 128)
            dst = pcol.at[k - 2] if d[0] == 0 else pcor.at[k - 4]
            return [remote(pool2.at[rows, lanes], dst, ssem, rsem, d)]
        if d[1] == 0:
            h, rows = ROWS[a], shapes[a][0]
            first, land = (0, rows) if d[0] < 0 else (rows - h, -h)
            if a == 0:
                seeds = x33.reshape(h3 + 2 * OFF3, s3, c3)
                return [remote(seeds.at[OFF3 + first : OFF3 + first + h, 0:wd3],
                               seeds.at[OFF3 + land : OFF3 + land + h, 0:wd3], ssem, rsem, d)]
            return [remote(inputs[a].at[first : first + h],
                           bufs[a].at[off[a] + land : off[a] + land + h, 0 : shapes[a][1]], ssem, rsem, d)]
        side = 0 if d[1] < 0 else 1
        if d[0] == 0:
            return [remote(sides[a].at[side], side_in[a].at[side], ssem, rsem, d)]
        tiles, total = corner_tiles(a), sides[a].shape[1]
        first = 0 if d[0] < 0 else total - tiles
        return [remote(sides[a].at[side, first : first + tiles], corner_in[a].at[k - 4], ssem, rsem, d)]

    def sent_bytes(k):
        d = DIRS[k]
        total = 4 * 128 * (wd3 if d[1] == 0 else h3 if d[0] == 0 else 8)
        for a, (_, cols, c) in enumerate(shapes):
            if d[1] == 0:
                total += 2 * ROWS[a] * cols * c
            else:
                total += 2 * SIDE * c * (sides[a].shape[1] if d[0] == 0 else corner_tiles(a))
        return total

    def send(a, ks):
        for k in ks:
            @pl.when(reachable(axes, counts, DIRS[k], 1))
            def _():
                for c in messages(a, k):
                    c.start()

    def put(a, row, slot, tiles):
        count = tiles.shape[0]
        tiles = tiles.astype(BF16)
        if a == 0:
            for q in range(count):
                at = (OFF3 + row + q) * s3 + slot
                x33[at : at + SIDE, :] = tiles[q]
        else:
            bufs[a][off[a] + row : off[a] + row + count, slot : slot + SIDE, :] = tiles

    def receive(a):
        h, (rows, cols, c) = ROWS[a], shapes[a]
        for k in range(8):
            d = DIRS[k]
            first, count = {0: (0, rows), -1: (rows, h), 1: (-h, h)}[d[0]]
            side = 0 if d[1] < 0 else 1
            slot = cols if side == 0 else cols + SIDE

            @pl.when(reachable(axes, counts, d, -1))
            def _():
                for m in messages(a, k):
                    m.wait_recv()
                if d[1]:
                    tiles = side_in[a][side] if d[0] == 0 else corner_in[a][k - 4]
                    spread = unpacked(tiles.astype(F32), WIDTHS[a], side)
                    spread = spread[:count] if d[0] <= 0 else spread[spread.shape[0] - count :]
                    put(a, first, slot, spread)

            if a != 4:
                @pl.when(jnp.logical_not(reachable(axes, counts, d, -1)))
                def _():
                    if d[1]:
                        put(a, first, slot, jnp.zeros((count, SIDE, c), F32))
                    elif a == 0:
                        for q in range(count):
                            x33[(OFF3 + first + q) * s3 : (OFF3 + first + q) * s3 + wd3, :] = jnp.zeros((wd3, c), BF16)
                    else:
                        bufs[a][off[a] + first : off[a] + first + count, 0:cols, :] = jnp.zeros((count, cols, c), BF16)

    def pack(a, side):
        rows, cols, c = shapes[a]
        at = 0 if side == 0 else cols - SIDE
        if a == 0:
            tiles = jnp.stack([x33[(OFF3 + q) * s3 + at : (OFF3 + q) * s3 + at + SIDE, :] for q in range(rows)])
        else:
            tiles = bufs[a][off[a] : off[a] + rows, at : at + SIDE, :]
        sides[a][side] = packed(tiles.astype(F32), WIDTHS[a], side).astype(BF16)

    def send_all(a):
        send(a, (0, 1))
        if a not in (3, 4):
            own(a).wait()
        pack(a, 0)
        pack(a, 1)
        send(a, range(2, 8))

    send_all(1)
    others[0].wait()
    others[1].wait()
    others[5].wait()
    others[6].wait()
    weight3 = 2.0 * lin3v[...]
    weight2 = 2.0 * lin2v[...]

    for i in range(h3 // SEED_ROWS):
        for q in range(SEED_ROWS):
            p = p33[SEED_ROWS * i + q].astype(F32)
            t = t33[SEED_ROWS * i + q].astype(F32)
            seed = jnp.where(p > 0, injected(p, t, weight3), 0.0).astype(BF16)
            row = OFF3 + SEED_ROWS * i + q
            x33[row * s3 : row * s3 + wd3, :] = seed
            x33t[row * tight : row * tight + wd3, :] = seed

    pack(0, 0)
    pack(0, 1)
    send(0, (4, 5, 6, 7, 0, 1, 2, 3))
    send_all(2)
    def tightened(rows):
        right, left = rows[:, wd3 : wd3 + SIDE], rows[:, wd3 + SIDE :]
        near = lax.broadcasted_iota(jnp.int32, right.shape, 1) < SIDE // 2
        return jnp.concatenate([rows[:, :wd3], jnp.where(near, right, left)], axis=1)

    def masked_conv(x, w, p, y, first, rows, channels):
        o = conv_rows(x, w, first, rows, tight, channels)
        pre = tightened(p[first : first + rows].astype(F32))
        y[first * tight : (first + rows) * tight, :] = jnp.where(pre > 0, o, 0.0).astype(BF16).reshape(rows * tight, channels)

    others[2].wait()
    for j in range(wd3):
        pedge[0, j : j + 1, :] = p2[0:1, j * 128 : (j + 1) * 128]
        pedge[1, j : j + 1, :] = p2[h3 - 1 : h3, j * 128 : (j + 1) * 128]
    for j in range(wd3):
        for i0 in range(0, h3, 8):
            blk = p2[i0 : i0 + 8, j * 128 : (j + 1) * 128]
            for b in range(2):
                upp[pl.ds((OFFU + i0) * s2 + 2 * j + b, 8, stride=s2), :] = blk
    others[4].wait()
    taps = [k21v[tap * 64 : (tap + 1) * 64, :].astype(F32) for tap in range(9)]
    for dy in range(3):
        for half, (p, q) in enumerate(((0, 2), (1, 1))):
            both = jnp.concatenate([taps[3 * dy + p], taps[3 * dy + q]], axis=0)
            w21[dy * c2 : (dy + 1) * c2, half * 128 : (half + 1) * 128] = both.T.astype(BF16)
    for dx in range(3):
        for p in range(2):
            w22[(3 - 3 * p) * c2 : (4 - 3 * p) * c2, (2 * dx + p) * c2 : (2 * dx + p + 1) * c2] = jnp.zeros((c2, c2), BF16)

    def inject_at(row, count, slot, width):
        p = bufs[3][pl.ds(row, count), slot : slot + width, :].reshape(count * width, c2).astype(F32)
        t = bufs[4][pl.ds(row, count), slot : slot + width, :].reshape(count * width, c2).astype(F32)
        value = injected(p, t, weight2)
        for q in range(count):
            injs[pl.ds(pl.multiple_of((row + q) * s2 + slot, 16), width), :] = value[q * width : (q + 1) * width]

    own(3).wait()
    own(4).wait()

    @pl.loop(0, h2 // 4)
    def _(i):
        inject_at(OFF2 + 4 * i, 4, 0, wd2)

    others[3].wait()

    @pl.loop(0, wd2 // 2)
    def _(g):
        blk = p1[:, pl.ds(pl.multiple_of(g * 128, 128), 128)]
        for a in range(2):
            twice[pl.ds(g * 2 * h2 + a, h2, stride=2), :] = blk

    send(n, range(8))
    for a in (3, 4, 5):
        send_all(a)
    receive(0)
    for c in weights(0):
        c.wait()
    receive(1)
    near = lax.broadcasted_iota(jnp.int32, (SIDE, c3), 0) < SIDE // 2
    for r in range(OFF3 - 4, OFF3 + h3 + 4):
        if not OFF3 <= r < OFF3 + h3:
            x33t[r * tight : r * tight + wd3, :] = x33[r * s3 : r * s3 + wd3, :]
        ends = x33[r * s3 + wd3 : (r + 1) * s3, :].astype(F32)
        x33t[r * tight + wd3 : (r + 1) * tight, :] = jnp.where(near, ends[:SIDE], ends[SIDE:]).astype(BF16)
    masked_conv(x33t, w33, bufs[1], x32, OFF3 - 3, h3 + 6, c3)
    receive(2)
    for c in weights(1):
        c.wait()
    masked_conv(x32, w32, bufs[2], x31, OFF3 - 2, h3 + 4, c3)

    for k in range(8):
        @pl.when(reachable(axes, counts, DIRS[k], -1))
        def _():
            for m in messages(n, k):
                m.wait_recv()
    for b in range(2):
        upp[pl.ds((OFFU + h3) * s2 + b, wd3, stride=2), :] = prow[0]
        upp[pl.ds((OFFU - 1) * s2 + b, wd3, stride=2), :] = prow[1]
        for i0 in range(0, h3, 8):
            upp[pl.ds((OFFU + i0) * s2 + wd2 + b, 8, stride=s2), :] = pcol[0, i0 : i0 + 8]
            upp[pl.ds((OFFU + i0) * s2 + s2 - 2 + b, 8, stride=s2), :] = pcol[1, i0 : i0 + 8]
        upp[(OFFU + h3) * s2 + wd2 + b : (OFFU + h3) * s2 + wd2 + b + 1, :] = pcor[0, 0:1]
        upp[(OFFU + h3) * s2 + s2 - 2 + b : (OFFU + h3) * s2 + s2 - 2 + b + 1, :] = pcor[1, 0:1]
        upp[(OFFU - 1) * s2 + wd2 + b : (OFFU - 1) * s2 + wd2 + b + 1, :] = pcor[2, 7:8]
        upp[(OFFU - 1) * s2 + s2 - 2 + b : (OFFU - 1) * s2 + s2 - 2 + b + 1, :] = pcor[3, 7:8]

    receive(3)
    receive(4)
    receive(5)
    for c in weights(3):
        c.wait()
    for c in weights(2):
        c.wait()
    o = conv_rows(x31, w31, OFF3 - 1, h3 + 2, tight, c2)
    for q in range(h3 + 2):
        base = (OFFU - 1 + q) * s2
        for b in range(2):
            upy[pl.ds(base + b, wd3, stride=2), :] = o[q, :wd3]
            upy[pl.ds(base + wd2 + b, 4, stride=2), :] = o[q, wd3 : wd3 + 4]
            upy[pl.ds(base + s2 - 8 + b, 4, stride=2), :] = o[q, tight - 4 :]

    for q in range(0, h2 + 4, SIDE):
        inject_at(OFF2 - 2 + q, min(SIDE, h2 + 4 - q), wd2, 2 * SIDE)
    inject_at(OFF2 - 2, 2, 0, wd2)
    inject_at(OFF2 + h2, 2, 0, wd2)
    par = lax.broadcasted_iota(jnp.int32, (s2, 128), 0) % 2

    for half in range((h2 + 4) // 2):
        at = slice((half + OFFU - 1) * s2, (half + OFFU) * s2)
        y = upy[at, :]
        m = upp[at, :]
        for i in range(2):
            row = OFF2 - 2 + 2 * half + i
            here = slice(row * s2, (row + 1) * s2)
            p = bufs[3][row].astype(F32)
            arriving = jnp.where(m == par + 2 * i, y, 0.0) + injs[here, :]
            x22[here, :] = jnp.where(p > 0, arriving, 0.0).astype(BF16)

    first, rows = OFF2 - 1, h2 + 2
    o = conv_pairs(x22, w22, first, rows, s2, c2)
    for q in range(rows):
        pre = bufs[5][first + q].astype(F32)
        half = o[q // 2, :, (q % 2) * c2 : (q % 2 + 1) * c2]
        x21[(first + q) * s2 : (first + q + 1) * s2, :] = jnp.where(pre > 0, half, 0.0).astype(BF16)

    for k in range(8):
        @pl.when(reachable(axes, counts, DIRS[k], 1))
        def _():
            held = upy.at[0 : sent_bytes(k) // 512]
            remote(held, held, send_sem.at[k], recv_sem.at[0, k], DIRS[k]).wait_send()


def tail_kernel(h2, wd2, c2, x21, w21, twice, out, yt, res, out_sem):
    s2 = wd2 + 2 * SIDE
    rows = 8
    low = lax.broadcasted_iota(jnp.int32, (rows, wd2, 128), 2) < 64
    lane_low = lax.broadcasted_iota(jnp.int32, (2 * rows, 128), 1) < 64
    want = (lax.broadcasted_iota(jnp.int32, (2 * rows, 128), 0) % 2) * 2 + jnp.where(lane_low, 0, 1)
    parts = []

    def conv(i):
        first = OFF2 + i * rows
        lhs = [x21[(first + 1 - dy) * s2 : (first + 1 - dy + rows) * s2, :] for dy in range(3)]
        z = jnp.dot(jnp.concatenate(lhs, axis=1), w21[...], preferred_element_type=F32).reshape(rows, s2, 256)
        sides = z[:, :, :128]
        t = jnp.where(low, pltpu.roll(sides, s2 - 1, 1)[:, :wd2], pltpu.roll(sides, 1, 1)[:, :wd2])
        y = t + pltpu.roll(t, 64, 2) + z[:, :wd2, 128:]
        for q in range(rows):
            for j0 in range(0, wd2, 8):
                for a in range(2):
                    yt[i, pl.ds(j0 * PITCH + 2 * q + a, 8, stride=PITCH), :] = y[q, j0 : j0 + 8]

    def ship(i, here, side):
        lanes = slice(side * wd2 * 64, (side + 1) * wd2 * 64)
        parts.append(pltpu.make_async_copy(res.at[here, lanes], out.at[here, lanes], out_sem.at[i, side]))
        parts[-1].start()

    def select(i):
        here = slice(i * 2 * rows, (i + 1) * 2 * rows)
        for g in range(wd2 // 2):
            if g == wd2 // 4:
                ship(i, here, 0)
            m = twice[g * 2 * h2 + i * 2 * rows : g * 2 * h2 + (i + 1) * 2 * rows, :]
            turned = pltpu.roll(m, 64, 1)
            for e in range(2):
                y = yt[i, (2 * g + e) * PITCH : (2 * g + e) * PITCH + 2 * rows, :]
                sel = jnp.where(lane_low, m, turned) if e == 0 else jnp.where(lane_low, turned, m)
                res[here, (2 * g + e) * 128 : (2 * g + e + 1) * 128] = jnp.where(sel == want, y, 0.0).astype(BF16)
        ship(i, here, 1)

    steps = h2 // rows
    conv(0)
    for i in range(steps):
        if i + 1 < steps:
            conv(i + 1)
        select(i)
    for c in parts:
        c.wait()


def shards(axes, counts, relu21, relu22, relu31, relu32, relu33, target22, target33, pool1, pool2, lin2, lin3,
           k21, k22, k31, k32, k33):
    tensors = (relu33, target33, relu32, relu31, relu22, target22, relu21)
    shapes = tuple(t.shape for t in (relu33, relu32, relu31, relu22, target22, relu21))
    h3, wd3, c3 = relu33.shape
    h2, wd2, c2 = relu22.shape
    s3, s2 = wd3 + 2 * SIDE, wd2 + 2 * SIDE
    anywhere = pl.BlockSpec(memory_space=pltpu.HBM)
    vmem = pl.BlockSpec(memory_space=pltpu.VMEM)
    rows3, rows2 = h3 + 2 * OFF3, h2 + 2 * OFF2
    per = [SIDE // w for w in WIDTHS]
    scratch = [pltpu.VMEM((h3, wd3, c3), BF16)] * 2
    scratch += [pltpu.VMEM((rows3, s3, c3), BF16)] * 2 + [pltpu.VMEM((rows2, s2, c2), BF16)] * 3
    scratch += [pltpu.VMEM((2, s[0] // k, SIDE, s[2]), BF16) for s, k in zip(shapes, per)] * 2
    scratch += [pltpu.VMEM((4, -(-r // k), SIDE, s[2]), BF16) for s, k, r in zip(shapes, per, ROWS)]
    scratch += [pltpu.VMEM((rows3 * s3, c3), BF16)] + [pltpu.VMEM((rows3 * (wd3 + SIDE), c3), BF16)] * 3 + [pltpu.VMEM((rows2 * s2, c2), BF16)]
    scratch += [pltpu.VMEM((3 * k.shape[0], k.shape[1] // 3), BF16) for k in (k33, k32, k31)]
    scratch += [
        pltpu.VMEM((4 * c2, 6 * c2), BF16),
        pltpu.VMEM(k21.shape[::-1], BF16),
        pltpu.VMEM((1, c2), F32),
        pltpu.VMEM((1, c3), F32),
        pltpu.VMEM(pool1.shape, jnp.int32),
        pltpu.VMEM(pool2.shape, jnp.int32),
        pltpu.VMEM((2, wd3, 128), jnp.int32),
        pltpu.VMEM((2, wd3, 128), jnp.int32),
        pltpu.VMEM((2, h3, 128), jnp.int32),
        pltpu.VMEM((4, 8, 128), jnp.int32),
        pltpu.VMEM(((h3 + 2 * OFFU + 1) * s2, 128), F32),
        pltpu.VMEM(((h3 + 2 * OFFU + 1) * s2, 128), jnp.int32),
        pltpu.VMEM((rows2 * s2, c2), F32),
        pltpu.SemaphoreType.DMA((6,)),
        pltpu.SemaphoreType.DMA((3, 3)),
        pltpu.SemaphoreType.DMA((2, 9)),
        pltpu.SemaphoreType.DMA((7,)),
        pltpu.SemaphoreType.DMA((8,)),
        pltpu.SemaphoreType.DMA((7, 8)),
    ]
    x21, w21, twice = pl.pallas_call(
        functools.partial(body_kernel, axes, counts, shapes),
        out_shape=[pltpu.VMEM((rows2 * s2, c2), BF16), pltpu.VMEM((3 * c2, 256), BF16), pltpu.VMEM((wd2 * h2, 128), jnp.int32)],
        in_specs=[anywhere] * 16,
        out_specs=[vmem] * 3,
        scratch_shapes=scratch,
        compiler_params=pltpu.CompilerParams(
            vmem_limit_bytes=40 * 1024 * 1024, collective_id=0, has_side_effects=True),
        name="body",
    )(*(pltpu.with_memory_space_constraint(v, pltpu.HBM) for v in (*tensors, pool1, pool2, lin2.reshape(1, c2), lin3.reshape(1, c3),
                                                                       k21.T, k22, k31, k32, k33)))
    return pl.pallas_call(
        functools.partial(tail_kernel, h2, wd2, c2),
        out_shape=jax.ShapeDtypeStruct((2 * h2, wd2 * 128), BF16),
        in_specs=[vmem] * 3,
        out_specs=anywhere,
        scratch_shapes=[
            pltpu.VMEM((h2 // 8, wd2 * PITCH + 8, 128), F32),
            pltpu.VMEM((2 * h2, wd2 * 128), BF16),
            pltpu.SemaphoreType.DMA((h2 // 8, 2)),
        ],
        compiler_params=pltpu.CompilerParams(vmem_limit_bytes=16 * 1024 * 1024),
        name="tail",
    )(*(pltpu.with_memory_space_constraint(v, pltpu.VMEM) for v in (x21, w21, twice)))


def solution(mesh):
    axes = ("row", "col")
    counts = tuple(mesh.shape[a] for a in axes)
    cells = P("row", "col", None)
    in_specs = (cells,) * 7 + (P("row", "col"),) * 2 + (P(),) * 7
    return jax.shard_map(functools.partial(shards, axes, counts), mesh=mesh, in_specs=in_specs,
                         out_specs=P("row", "col"), check_vma=False)
```

```python
import functools

import jax
import jax.numpy as jnp
from jax import lax
from jax.experimental import pallas as pl
from jax.experimental.pallas import tpu as pltpu
from jax.sharding import PartitionSpec as P

EPSILON = 1e-06
MESH = pl.DeviceIdType.MESH
F32 = jnp.float32
BF16 = jnp.bfloat16
SIDE = 8
OFF3 = 6
OFF2 = 4
OFFU = 2
SEED_ROWS = 4
PITCH = 17
DIRS = ((-1, 0), (1, 0), (0, -1), (0, 1), (-1, -1), (-1, 1), (1, -1), (1, 1))


WIDTHS = (4, 4, 2, 2, 2, 1)
ROWS = (4, 3, 2, 2, 2, 1)


def reachable(axes, counts, d, sign):
    checks = []
    for axis, count, step in zip(axes, counts, d):
        if step:
            target = lax.axis_index(axis) + sign * step
            checks.append(target >= 0 if sign * step < 0 else target < count)
    ok = checks[0]
    for c in checks[1:]:
        ok = jnp.logical_and(ok, c)
    return ok


def packed(tiles, width, side):
    k = SIDE // width
    rows, _, c = tiles.shape
    grouped = tiles.reshape(rows // k, k, SIDE, c)
    sub = lax.broadcasted_iota(jnp.int32, (rows // k, SIDE, c), 1)
    total = None
    for i in range(k):
        shift = (i * width - (0 if side == 0 else SIDE - width)) % SIDE
        piece = grouped[:, i]
        if shift:
            piece = pltpu.roll(piece, shift, 1)
        total = piece if total is None else jnp.where(sub >= i * width, piece, total)
    return total


def unpacked(tiles, width, side):
    k = SIDE // width
    count, _, c = tiles.shape
    pieces = []
    for i in range(k):
        shift = ((0 if side == 0 else SIDE - width) - i * width) % SIDE
        pieces.append(pltpu.roll(tiles, shift, 1) if shift else tiles)
    return jnp.stack(pieces, axis=1).reshape(count * k, SIDE, c)


def injected(p, t, weight):
    n = p.shape[-1]
    f = jnp.maximum(p, 0.0)
    g = jnp.maximum(t, 0.0)
    wf = weight * f
    ff = jnp.sum(f * f, axis=-1, keepdims=True)
    gg = jnp.sum(g * g, axis=-1, keepdims=True)
    wff = jnp.sum(wf * f, axis=-1, keepdims=True)
    wfg = jnp.sum(wf * g, axis=-1, keepdims=True)
    rinv = lax.rsqrt(ff * (1.0 / n) + EPSILON)
    both = rinv * lax.rsqrt(gg * (1.0 / n) + EPSILON)
    own = rinv * rinv
    level = (own * wff - both * wfg) * (1.0 / n)
    return own * (wf - level * f) - both * (weight * g)


def row_shifts(z, stride, n):
    z = z.reshape(-1, stride, 3 * n)
    return pltpu.roll(z[:, :, :n], stride - 1, 1) + z[:, :, n : 2 * n] + pltpu.roll(z[:, :, 2 * n :], 1, 1)


def conv_rows(x, w, first, rows, stride, n):
    half = rows // 2
    def part(at):
        parts = [x[(at + 1 - dy) * stride : (at + 1 - dy + half) * stride, :] for dy in range(3)]
        z = jnp.dot(jnp.concatenate(parts, axis=1), w[...], preferred_element_type=F32)
        return row_shifts(z, stride, n)
    return jnp.concatenate([part(first), part(first + half)], axis=0)


def conv_pairs(x, w, first, rows, stride, n):
    def part(at, count):
        parts = [jnp.concatenate([x[(at + q + j - 1) * stride : (at + q + j) * stride, :] for q in range(0, count, 2)], axis=0)
                 for j in range(4)]
        z = jnp.dot(jnp.concatenate(parts, axis=1), w[...], preferred_element_type=F32)
        return row_shifts(z, stride, 2 * n)

    half = rows // 4 * 2
    return jnp.concatenate([part(first, half), part(first + half, rows - half)], axis=0)


def body_kernel(axes, counts, shapes, *refs):
    (relu33, target33, relu32, relu31, relu22, target22, relu21,
     pool1, pool2, lin2, lin3, k21, k22, k31, k32, k33, x21, w21, twice) = refs[:19]
    scratch = refs[19:]
    inputs = (None, relu32, relu31, relu22, target22, relu21)
    p33, t33 = scratch[:2]
    bufs = (None,) + tuple(scratch[2:7])
    sides, side_in, corner_in = scratch[7:13], scratch[13:19], scratch[19:25]
    (x33, x33t, x32, x31, x22, w33, w32, w31, w22, k21v, lin2v, lin3v, p1, p2, pedge, prow, pcol, pcor, upy, upp, injs,
     own_sem, w_sem, pair_sem, misc_sem, send_sem, recv_sem) = scratch[25:]
    n = 6
    off = [OFF3, OFF3, OFF3, OFF2, OFF2, OFF2]
    h3, wd3, c3 = shapes[0]
    h2, wd2, c2 = shapes[3]
    s3, s2 = wd3 + 2 * SIDE, wd2 + 2 * SIDE
    tight = wd3 + SIDE

    def own(a):
        return pltpu.make_async_copy(
            inputs[a], bufs[a].at[off[a] : off[a] + shapes[a][0], 0 : shapes[a][1]], own_sem.at[a])

    def weights(i):
        if i == 3:
            return [pltpu.make_async_copy(
                k22.at[:, tap * c2 : (tap + 1) * c2],
                w22.at[(p + 2 - tap // 3) * c2 : (p + 3 - tap // 3) * c2, (2 * (tap % 3) + p) * c2 : (2 * (tap % 3) + p + 1) * c2],
                pair_sem.at[p, tap]) for p in range(2) for tap in range(9)]
        k, w = ((k33, w33), (k32, w32), (k31, w31))[i]
        o, cols = k.shape[0], k.shape[1] // 3
        return [pltpu.make_async_copy(k.at[:, dy * cols : (dy + 1) * cols], w.at[dy * o : (dy + 1) * o], w_sem.at[i, dy])
                for dy in range(3)]

    others = [pltpu.make_async_copy(src, dst, misc_sem.at[i])
              for i, (src, dst) in enumerate(((relu33, p33), (target33, t33), (pool2, p2), (pool1, p1), (k21, k21v), (lin3, lin3v), (lin2, lin2v)))]
    others[0].start()
    others[1].start()
    others[5].start()
    others[6].start()
    for a in (1, 2, 3, 4, 5):
        own(a).start()
    others[2].start()
    for i in range(4):
        for c in weights(i):
            c.start()
    others[4].start()
    others[3].start()

    me = tuple(lax.axis_index(axis) for axis in axes)

    def peer(d):
        return (me[0] + d[0], me[1] + d[1])

    barrier = pltpu.get_barrier_semaphore()
    for d in DIRS:
        @pl.when(reachable(axes, counts, d, 1))
        def _():
            pl.semaphore_signal(barrier, inc=1, device_id=peer(d), device_id_type=MESH)
    spans = [1 + jnp.minimum(m, 1) + jnp.minimum(c - 1 - m, 1) for m, c in zip(me, counts)]
    pl.semaphore_wait(barrier, spans[0] * spans[1] - 1)

    def remote(src, dst, ssem, rsem, d):
        return pltpu.make_async_remote_copy(
            src_ref=src, dst_ref=dst, send_sem=ssem, recv_sem=rsem, device_id=peer(d), device_id_type=MESH)

    def corner_tiles(a):
        k = SIDE // WIDTHS[a]
        return -(-ROWS[a] // k)

    def messages(a, k):
        d = DIRS[k]
        ssem, rsem = send_sem.at[k], recv_sem.at[a, k]
        if a == n:
            if d[1] == 0:
                return [remote(pedge.at[k], prow.at[k], ssem, rsem, d)]
            rows = {0: slice(0, h3), -1: slice(0, 8), 1: slice(h3 - 8, h3)}[d[0]]
            lanes = slice(0, 128) if d[1] < 0 else slice((wd3 - 1) * 128, wd3 * 128)
            dst = pcol.at[k - 2] if d[0] == 0 else pcor.at[k - 4]
            return [remote(pool2.at[rows, lanes], dst, ssem, rsem, d)]
        if d[1] == 0:
            h, rows = ROWS[a], shapes[a][0]
            first, land = (0, rows) if d[0] < 0 else (rows - h, -h)
            if a == 0:
                seeds = x33.reshape(h3 + 2 * OFF3, s3, c3)
                return [remote(seeds.at[OFF3 + first : OFF3 + first + h, 0:wd3],
                               seeds.at[OFF3 + land : OFF3 + land + h, 0:wd3], ssem, rsem, d)]
            return [remote(inputs[a].at[first : first + h],
                           bufs[a].at[off[a] + land : off[a] + land + h, 0 : shapes[a][1]], ssem, rsem, d)]
        side = 0 if d[1] < 0 else 1
        if d[0] == 0:
            return [remote(sides[a].at[side], side_in[a].at[side], ssem, rsem, d)]
        tiles, total = corner_tiles(a), sides[a].shape[1]
        first = 0 if d[0] < 0 else total - tiles
        return [remote(sides[a].at[side, first : first + tiles], corner_in[a].at[k - 4], ssem, rsem, d)]

    def sent_bytes(k):
        d = DIRS[k]
        total = 4 * 128 * (wd3 if d[1] == 0 else h3 if d[0] == 0 else 8)
        for a, (_, cols, c) in enumerate(shapes):
            if d[1] == 0:
                total += 2 * ROWS[a] * cols * c
            else:
                total += 2 * SIDE * c * (sides[a].shape[1] if d[0] == 0 else corner_tiles(a))
        return total

    def send(a, ks):
        for k in ks:
            @pl.when(reachable(axes, counts, DIRS[k], 1))
            def _():
                for c in messages(a, k):
                    c.start()

    def put(a, row, slot, tiles):
        count = tiles.shape[0]
        tiles = tiles.astype(BF16)
        if a == 0:
            for q in range(count):
                at = (OFF3 + row + q) * s3 + slot
                x33[at : at + SIDE, :] = tiles[q]
        else:
            bufs[a][off[a] + row : off[a] + row + count, slot : slot + SIDE, :] = tiles

    def receive(a):
        h, (rows, cols, c) = ROWS[a], shapes[a]
        for k in range(8):
            d = DIRS[k]
            first, count = {0: (0, rows), -1: (rows, h), 1: (-h, h)}[d[0]]
            side = 0 if d[1] < 0 else 1
            slot = cols if side == 0 else cols + SIDE

            @pl.when(reachable(axes, counts, d, -1))
            def _():
                for m in messages(a, k):
                    m.wait_recv()
                if d[1]:
                    tiles = side_in[a][side] if d[0] == 0 else corner_in[a][k - 4]
                    spread = unpacked(tiles.astype(F32), WIDTHS[a], side)
                    spread = spread[:count] if d[0] <= 0 else spread[spread.shape[0] - count :]
                    put(a, first, slot, spread)

            if a != 4:
                @pl.when(jnp.logical_not(reachable(axes, counts, d, -1)))
                def _():
                    if d[1]:
                        put(a, first, slot, jnp.zeros((count, SIDE, c), F32))
                    elif a == 0:
                        for q in range(count):
                            x33[(OFF3 + first + q) * s3 : (OFF3 + first + q) * s3 + wd3, :] = jnp.zeros((wd3, c), BF16)
                    else:
                        bufs[a][off[a] + first : off[a] + first + count, 0:cols, :] = jnp.zeros((count, cols, c), BF16)

    def pack(a, side):
        rows, cols, c = shapes[a]
        at = 0 if side == 0 else cols - SIDE
        if a == 0:
            tiles = jnp.stack([x33[(OFF3 + q) * s3 + at : (OFF3 + q) * s3 + at + SIDE, :] for q in range(rows)])
        else:
            tiles = bufs[a][off[a] : off[a] + rows, at : at + SIDE, :]
        sides[a][side] = packed(tiles.astype(F32), WIDTHS[a], side).astype(BF16)

    def send_all(a):
        send(a, (0, 1))
        if a not in (3, 4):
            own(a).wait()
        pack(a, 0)
        pack(a, 1)
        send(a, range(2, 8))

    others[0].wait()
    others[1].wait()
    others[5].wait()
    others[6].wait()
    weight3 = 2.0 * lin3v[...]
    weight2 = 2.0 * lin2v[...]

    for i in range(h3 // SEED_ROWS):
        for q in range(SEED_ROWS):
            p = p33[SEED_ROWS * i + q].astype(F32)
            t = t33[SEED_ROWS * i + q].astype(F32)
            seed = jnp.where(p > 0, injected(p, t, weight3), 0.0).astype(BF16)
            row = OFF3 + SEED_ROWS * i + q
            x33[row * s3 : row * s3 + wd3, :] = seed
            x33t[row * tight : row * tight + wd3, :] = seed

    pack(0, 0)
    pack(0, 1)
    send(0, (4, 5, 6, 7, 0, 1, 2, 3))
    send_all(1)
    send_all(2)
    def tightened(rows):
        right, left = rows[:, wd3 : wd3 + SIDE], rows[:, wd3 + SIDE :]
        near = lax.broadcasted_iota(jnp.int32, right.shape, 1) < SIDE // 2
        return jnp.concatenate([rows[:, :wd3], jnp.where(near, right, left)], axis=1)

    def masked_conv(x, w, p, y, first, rows, channels):
        o = conv_rows(x, w, first, rows, tight, channels)
        pre = tightened(p[first : first + rows].astype(F32))
        y[first * tight : (first + rows) * tight, :] = jnp.where(pre > 0, o, 0.0).astype(BF16).reshape(rows * tight, channels)

    others[2].wait()
    for j in range(wd3):
        pedge[0, j : j + 1, :] = p2[0:1, j * 128 : (j + 1) * 128]
        pedge[1, j : j + 1, :] = p2[h3 - 1 : h3, j * 128 : (j + 1) * 128]
    for j in range(wd3):
        for i0 in range(0, h3, 8):
            blk = p2[i0 : i0 + 8, j * 128 : (j + 1) * 128]
            for b in range(2):
                upp[pl.ds((OFFU + i0) * s2 + 2 * j + b, 8, stride=s2), :] = blk
    others[4].wait()
    taps = [k21v[tap * 64 : (tap + 1) * 64, :].astype(F32) for tap in range(9)]
    for dy in range(3):
        for half, (p, q) in enumerate(((0, 2), (1, 1))):
            both = jnp.concatenate([taps[3 * dy + p], taps[3 * dy + q]], axis=0)
            w21[dy * c2 : (dy + 1) * c2, half * 128 : (half + 1) * 128] = both.T.astype(BF16)
    for dx in range(3):
        for p in range(2):
            w22[(3 - 3 * p) * c2 : (4 - 3 * p) * c2, (2 * dx + p) * c2 : (2 * dx + p + 1) * c2] = jnp.zeros((c2, c2), BF16)

    def inject_at(row, count, slot, width):
        p = bufs[3][pl.ds(row, count), slot : slot + width, :].reshape(count * width, c2).astype(F32)
        t = bufs[4][pl.ds(row, count), slot : slot + width, :].reshape(count * width, c2).astype(F32)
        value = injected(p, t, weight2)
        for q in range(count):
            injs[pl.ds(pl.multiple_of((row + q) * s2 + slot, 16), width), :] = value[q * width : (q + 1) * width]

    own(3).wait()
    own(4).wait()

    @pl.loop(0, h2 // 4)
    def _(i):
        inject_at(OFF2 + 4 * i, 4, 0, wd2)

    others[3].wait()

    @pl.loop(0, wd2 // 2)
    def _(g):
        blk = p1[:, pl.ds(pl.multiple_of(g * 128, 128), 128)]
        for a in range(2):
            twice[pl.ds(g * 2 * h2 + a, h2, stride=2), :] = blk

    send(n, range(8))
    for a in (3, 4, 5):
        send_all(a)
    receive(0)
    for c in weights(0):
        c.wait()
    receive(1)
    near = lax.broadcasted_iota(jnp.int32, (SIDE, c3), 0) < SIDE // 2
    for r in range(OFF3 - 4, OFF3 + h3 + 4):
        if not OFF3 <= r < OFF3 + h3:
            x33t[r * tight : r * tight + wd3, :] = x33[r * s3 : r * s3 + wd3, :]
        ends = x33[r * s3 + wd3 : (r + 1) * s3, :].astype(F32)
        x33t[r * tight + wd3 : (r + 1) * tight, :] = jnp.where(near, ends[:SIDE], ends[SIDE:]).astype(BF16)
    masked_conv(x33t, w33, bufs[1], x32, OFF3 - 3, h3 + 6, c3)
    receive(2)
    for c in weights(1):
        c.wait()
    masked_conv(x32, w32, bufs[2], x31, OFF3 - 2, h3 + 4, c3)

    for k in range(8):
        @pl.when(reachable(axes, counts, DIRS[k], -1))
        def _():
            for m in messages(n, k):
                m.wait_recv()
    for b in range(2):
        upp[pl.ds((OFFU + h3) * s2 + b, wd3, stride=2), :] = prow[0]
        upp[pl.ds((OFFU - 1) * s2 + b, wd3, stride=2), :] = prow[1]
        for i0 in range(0, h3, 8):
            upp[pl.ds((OFFU + i0) * s2 + wd2 + b, 8, stride=s2), :] = pcol[0, i0 : i0 + 8]
            upp[pl.ds((OFFU + i0) * s2 + s2 - 2 + b, 8, stride=s2), :] = pcol[1, i0 : i0 + 8]
        upp[(OFFU + h3) * s2 + wd2 + b : (OFFU + h3) * s2 + wd2 + b + 1, :] = pcor[0, 0:1]
        upp[(OFFU + h3) * s2 + s2 - 2 + b : (OFFU + h3) * s2 + s2 - 2 + b + 1, :] = pcor[1, 0:1]
        upp[(OFFU - 1) * s2 + wd2 + b : (OFFU - 1) * s2 + wd2 + b + 1, :] = pcor[2, 7:8]
        upp[(OFFU - 1) * s2 + s2 - 2 + b : (OFFU - 1) * s2 + s2 - 2 + b + 1, :] = pcor[3, 7:8]

    receive(3)
    receive(4)
    receive(5)
    for c in weights(3):
        c.wait()
    for c in weights(2):
        c.wait()
    o = conv_rows(x31, w31, OFF3 - 1, h3 + 2, tight, c2)
    for q in range(h3 + 2):
        base = (OFFU - 1 + q) * s2
        for b in range(2):
            upy[pl.ds(base + b, wd3, stride=2), :] = o[q, :wd3]
            upy[pl.ds(base + wd2 + b, 4, stride=2), :] = o[q, wd3 : wd3 + 4]
            upy[pl.ds(base + s2 - 8 + b, 4, stride=2), :] = o[q, tight - 4 :]

    for q in range(0, h2 + 4, SIDE):
        inject_at(OFF2 - 2 + q, min(SIDE, h2 + 4 - q), wd2, 2 * SIDE)
    inject_at(OFF2 - 2, 2, 0, wd2)
    inject_at(OFF2 + h2, 2, 0, wd2)
    par = lax.broadcasted_iota(jnp.int32, (s2, 128), 0) % 2

    for half in range((h2 + 4) // 2):
        at = slice((half + OFFU - 1) * s2, (half + OFFU) * s2)
        y = upy[at, :]
        m = upp[at, :]
        for i in range(2):
            row = OFF2 - 2 + 2 * half + i
            here = slice(row * s2, (row + 1) * s2)
            p = bufs[3][row].astype(F32)
            arriving = jnp.where(m == par + 2 * i, y, 0.0) + injs[here, :]
            x22[here, :] = jnp.where(p > 0, arriving, 0.0).astype(BF16)

    first, rows = OFF2 - 1, h2 + 2
    o = conv_pairs(x22, w22, first, rows, s2, c2)
    for q in range(rows):
        pre = bufs[5][first + q].astype(F32)
        half = o[q // 2, :, (q % 2) * c2 : (q % 2 + 1) * c2]
        x21[(first + q) * s2 : (first + q + 1) * s2, :] = jnp.where(pre > 0, half, 0.0).astype(BF16)

    for k in range(8):
        @pl.when(reachable(axes, counts, DIRS[k], 1))
        def _():
            held = upy.at[0 : sent_bytes(k) // 512]
            remote(held, held, send_sem.at[k], recv_sem.at[0, k], DIRS[k]).wait_send()


def tail_kernel(h2, wd2, c2, x21, w21, twice, out, yt, res, out_sem):
    s2 = wd2 + 2 * SIDE
    rows = 8
    low = lax.broadcasted_iota(jnp.int32, (rows, wd2, 128), 2) < 64
    lane_low = lax.broadcasted_iota(jnp.int32, (2 * rows, 128), 1) < 64
    want = (lax.broadcasted_iota(jnp.int32, (2 * rows, 128), 0) % 2) * 2 + jnp.where(lane_low, 0, 1)
    parts = []

    def conv(i):
        first = OFF2 + i * rows
        lhs = [x21[(first + 1 - dy) * s2 : (first + 1 - dy + rows) * s2, :] for dy in range(3)]
        z = jnp.dot(jnp.concatenate(lhs, axis=1), w21[...], preferred_element_type=F32).reshape(rows, s2, 256)
        sides = z[:, :, :128]
        t = jnp.where(low, pltpu.roll(sides, s2 - 1, 1)[:, :wd2], pltpu.roll(sides, 1, 1)[:, :wd2])
        y = t + pltpu.roll(t, 64, 2) + z[:, :wd2, 128:]
        for q in range(rows):
            for j0 in range(0, wd2, 8):
                for a in range(2):
                    yt[i, pl.ds(j0 * PITCH + 2 * q + a, 8, stride=PITCH), :] = y[q, j0 : j0 + 8]

    def ship(i, here, side):
        lanes = slice(side * wd2 * 64, (side + 1) * wd2 * 64)
        parts.append(pltpu.make_async_copy(res.at[here, lanes], out.at[here, lanes], out_sem.at[i, side]))
        parts[-1].start()

    def select(i):
        here = slice(i * 2 * rows, (i + 1) * 2 * rows)
        for g in range(wd2 // 2):
            if g == wd2 // 4:
                ship(i, here, 0)
            m = twice[g * 2 * h2 + i * 2 * rows : g * 2 * h2 + (i + 1) * 2 * rows, :]
            turned = pltpu.roll(m, 64, 1)
            for e in range(2):
                y = yt[i, (2 * g + e) * PITCH : (2 * g + e) * PITCH + 2 * rows, :]
                sel = jnp.where(lane_low, m, turned) if e == 0 else jnp.where(lane_low, turned, m)
                res[here, (2 * g + e) * 128 : (2 * g + e + 1) * 128] = jnp.where(sel == want, y, 0.0).astype(BF16)
        ship(i, here, 1)

    steps = h2 // rows
    conv(0)
    for i in range(steps):
        if i + 1 < steps:
            conv(i + 1)
        select(i)
    for c in parts:
        c.wait()


def shards(axes, counts, relu21, relu22, relu31, relu32, relu33, target22, target33, pool1, pool2, lin2, lin3,
           k21, k22, k31, k32, k33):
    tensors = (relu33, target33, relu32, relu31, relu22, target22, relu21)
    shapes = tuple(t.shape for t in (relu33, relu32, relu31, relu22, target22, relu21))
    h3, wd3, c3 = relu33.shape
    h2, wd2, c2 = relu22.shape
    s3, s2 = wd3 + 2 * SIDE, wd2 + 2 * SIDE
    anywhere = pl.BlockSpec(memory_space=pltpu.HBM)
    vmem = pl.BlockSpec(memory_space=pltpu.VMEM)
    rows3, rows2 = h3 + 2 * OFF3, h2 + 2 * OFF2
    per = [SIDE // w for w in WIDTHS]
    scratch = [pltpu.VMEM((h3, wd3, c3), BF16)] * 2
    scratch += [pltpu.VMEM((rows3, s3, c3), BF16)] * 2 + [pltpu.VMEM((rows2, s2, c2), BF16)] * 3
    scratch += [pltpu.VMEM((2, s[0] // k, SIDE, s[2]), BF16) for s, k in zip(shapes, per)] * 2
    scratch += [pltpu.VMEM((4, -(-r // k), SIDE, s[2]), BF16) for s, k, r in zip(shapes, per, ROWS)]
    scratch += [pltpu.VMEM((rows3 * s3, c3), BF16)] + [pltpu.VMEM((rows3 * (wd3 + SIDE), c3), BF16)] * 3 + [pltpu.VMEM((rows2 * s2, c2), BF16)]
    scratch += [pltpu.VMEM((3 * k.shape[0], k.shape[1] // 3), BF16) for k in (k33, k32, k31)]
    scratch += [
        pltpu.VMEM((4 * c2, 6 * c2), BF16),
        pltpu.VMEM(k21.shape[::-1], BF16),
        pltpu.VMEM((1, c2), F32),
        pltpu.VMEM((1, c3), F32),
        pltpu.VMEM(pool1.shape, jnp.int32),
        pltpu.VMEM(pool2.shape, jnp.int32),
        pltpu.VMEM((2, wd3, 128), jnp.int32),
        pltpu.VMEM((2, wd3, 128), jnp.int32),
        pltpu.VMEM((2, h3, 128), jnp.int32),
        pltpu.VMEM((4, 8, 128), jnp.int32),
        pltpu.VMEM(((h3 + 2 * OFFU + 1) * s2, 128), F32),
        pltpu.VMEM(((h3 + 2 * OFFU + 1) * s2, 128), jnp.int32),
        pltpu.VMEM((rows2 * s2, c2), F32),
        pltpu.SemaphoreType.DMA((6,)),
        pltpu.SemaphoreType.DMA((3, 3)),
        pltpu.SemaphoreType.DMA((2, 9)),
        pltpu.SemaphoreType.DMA((7,)),
        pltpu.SemaphoreType.DMA((8,)),
        pltpu.SemaphoreType.DMA((7, 8)),
    ]
    x21, w21, twice = pl.pallas_call(
        functools.partial(body_kernel, axes, counts, shapes),
        out_shape=[pltpu.VMEM((rows2 * s2, c2), BF16), pltpu.VMEM((3 * c2, 256), BF16), pltpu.VMEM((wd2 * h2, 128), jnp.int32)],
        in_specs=[anywhere] * 16,
        out_specs=[vmem] * 3,
        scratch_shapes=scratch,
        compiler_params=pltpu.CompilerParams(
            vmem_limit_bytes=40 * 1024 * 1024, collective_id=0, has_side_effects=True),
        name="body",
    )(*(pltpu.with_memory_space_constraint(v, pltpu.HBM) for v in (*tensors, pool1, pool2, lin2.reshape(1, c2), lin3.reshape(1, c3),
                                                                       k21.T, k22, k31, k32, k33)))
    return pl.pallas_call(
        functools.partial(tail_kernel, h2, wd2, c2),
        out_shape=jax.ShapeDtypeStruct((2 * h2, wd2 * 128), BF16),
        in_specs=[vmem] * 3,
        out_specs=anywhere,
        scratch_shapes=[
            pltpu.VMEM((h2 // 8, wd2 * PITCH + 8, 128), F32),
            pltpu.VMEM((2 * h2, wd2 * 128), BF16),
            pltpu.SemaphoreType.DMA((h2 // 8, 2)),
        ],
        compiler_params=pltpu.CompilerParams(vmem_limit_bytes=16 * 1024 * 1024),
        name="tail",
    )(*(pltpu.with_memory_space_constraint(v, pltpu.VMEM) for v in (x21, w21, twice)))


def solution(mesh):
    axes = ("row", "col")
    counts = tuple(mesh.shape[a] for a in axes)
    cells = P("row", "col", None)
    in_specs = (cells,) * 7 + (P("row", "col"),) * 2 + (P(),) * 7
    return jax.shard_map(functools.partial(shards, axes, counts), mesh=mesh, in_specs=in_specs,
                         out_specs=P("row", "col"), check_vma=False)
```
